512 devices in a mesh: expert: 8 (over y, x_lo), dp: 64 (over z, x_hi, core).
Axes of the slice: x: 4 (x_hi: 2, x_lo: 2; x = x_hi * 2 + x_lo), y: 4, z: 16, core: 2. Of those that a mesh axis runs over, the one named last changes fastest.
Arguments:
- x_new: bfloat16 [512, 4096], P('expert', 'dp'), may hold values from -6 to 6
- routes_new: int32 [512, 2], P('expert'), may hold values from 0 to 7, all different within a row; in each aligned block of 64 rows (0 to 63, 64 to 127, ...) at most 32 rows name the same one
- gates_new: float32 [512, 2], P('expert'), may hold values from 0.2 to 1
- w_gate: bfloat16 [8, 4096, 7168], P('expert', None, 'dp'), may hold values from -0.09375 to 0.09375
- w_up: bfloat16 [8, 4096, 7168], P('expert', None, 'dp'), may hold values from -0.09375 to 0.09375
- w_down: bfloat16 [8, 7168, 4096], P('expert', 'dp'), may hold values from -0.1875 to 0.1875
- grad_out: bfloat16 [1024, 4096], P('expert', 'dp'), may hold values from -6 to 6
- routes_old: int32 [1024, 2], P('expert'), may hold values from 0 to 7, all different within a row; in each aligned block of 128 rows (0 to 127, 128 to 255, ...) at most 64 rows name the same one
- gates_old: float32 [1024, 2], P('expert'), may hold values from 0.2 to 1
- pre_gate: bfloat16 [8, 512, 7168], P('expert', None, 'dp'), may hold values from -8 to 8
- pre_up: bfloat16 [8, 512, 7168], P('expert', None, 'dp'), may hold values from -6 to 6
Outputs:
- mixed: bfloat16 [512, 4096], P('expert', 'dp')
- grad_down: bfloat16 [8, 7168, 4096], P('expert', 'dp')
- grad_gate: bfloat16 [8, 512, 7168], P('expert', None, 'dp')
- grad_up: bfloat16 [8, 512, 7168], P('expert', None, 'dp')
The draws below stay inside these ranges and needn't reach their ends.
Inputs may be any that keep to these rules, and one draw needn't show every extreme that they name: `routes_new`: in each group of 64 tokens each expert is named by at most 32 tokens, and by exactly 32 tokens in some group; the two experts of a token differ. `routes_old`: in each group of 128 tokens each expert is named by at most 64 tokens, and by exactly 64 tokens in some group; the two experts of a token differ.
All inputs are finite; a program needn't handle non-finite values.
Results may differ from the reference program's by a relative error of at most 0.0078.
Values may be sent and summed in bfloat16 or wider, within the bound.
No kernel may reach another device: no remote copies, remote signals or barrier semaphores. Data moves between devices by JAX's collectives and lax.ppermute only.
A program may use at most 64 MiB of HBM per device.

```python
import math
import jax
import jax.numpy as jnp
import numpy as np
from jax import lax

D = 4096
FF = 7168
CAP_B = 32
CAP_A = 64
EXPERTS = 8
TOK_B = 64
TOK_A = 128
TOKENS_B = 512
TOKENS_A = 1024


def raised(drawn, key, source, target, parts, factor):
    def block_of(dim):
        return (jnp.arange(drawn.shape[dim]) // (drawn.shape[dim] // parts)).reshape((-1,) + (1,) * (drawn.ndim - 1 - dim))

    near = jax.random.permutation(key, parts)[block_of(target)]
    other_side = (block_of(target) + parts // 2) % parts
    return jnp.where((block_of(source) == near) | (block_of(source) == other_side), factor * drawn, drawn)


def shard_levels(key, shape, cuts, least, largest):
    factor_of, own = 1.0, jax.random.fold_in(key, 6)
    for dim, parts in cuts:
        draws = jnp.exp(jax.random.uniform(jax.random.fold_in(own, dim), (parts,), jnp.float32, least / len(cuts), largest / len(cuts)))
        factor_of = factor_of * jnp.repeat(draws, shape[dim] // parts).reshape([-1 if axis == dim else 1 for axis in range(len(shape))])
    return factor_of


def assign_block(stream_key, own, number, rows, count, top, bound, skew):
    order = jax.random.permutation(stream_key, count)
    packed, common = portions_of(count, rows * top, bound, skew, True), portions_of(count, rows * top, bound, skew, False)
    places = jnp.arange(count)

    def named(sizes, offset_by):
        used = int((sizes > 0).sum())
        fixed = max(1, used // 4)
        passed = fixed + (places - fixed + offset_by * (used - fixed)) % max(1, count - fixed)
        return jnp.zeros((count,), jnp.int32).at[order[jnp.where(places < fixed, places, passed)]].set(jnp.asarray(sizes, jnp.int32))

    sizes = jnp.where(number % 4 == 0, named(packed, number // 4), named(common, number - number // 4 - 1))
    mixed = jax.random.permutation(jax.random.fold_in(own, 3), count)
    donor, receiver = mixed[0:count // 2 * 2:2], mixed[1:count // 2 * 2:2]
    margin = jnp.minimum(sizes[donor] - 1, bound - sizes[receiver]) // 2
    margin = jnp.where((donor == order[0]) | (receiver == order[0]) | (sizes[receiver] == 0), 0, jnp.maximum(margin, 0))
    passed = jax.random.randint(jax.random.fold_in(own, 4), (count // 2,), 0, 1 << 20) % (margin + 1)
    sizes = sizes.at[donor].add(-passed).at[receiver].add(passed)
    labels = jnp.searchsorted(jnp.cumsum(sizes), jnp.arange(rows * top), side="right").astype(jnp.int32)
    table = labels.reshape(top, rows).T
    table = table[jax.random.permutation(jax.random.fold_in(own, 1), rows)]
    offset_by = jax.random.randint(jax.random.fold_in(own, 2), (rows, 1), 0, top)
    return jnp.take_along_axis(table, (jnp.arange(top)[None, :] + offset_by) % top, axis=1)


def portions_of(number_of, total, reach, skew, full):
    weights = [(1 << 20) // math.isqrt(grade ** skew) + 1 for grade in range(1, number_of + 1)]
    largest = reach if full else min(reach, max(-(-total // number_of), total * weights[0] // sum(weights)))
    least = 1 if total - largest >= number_of - 1 else 0
    holding, spare = [largest] + [least] * (number_of - 1), total - largest - least * (number_of - 1)
    while spare > 0:
        movable = [i for i in range(1, number_of) if holding[i] < largest] or [i for i in range(1, number_of) if holding[i] < reach]
        mass, budget = sum([weights[i] for i in movable]), spare
        for i in movable:
            addition = min(reach - holding[i], max(1, budget * weights[i] // mass), spare)
            holding[i] = holding[i] + addition
            spare = spare - addition
    return np.array(holding)


def scatter_about(stream_key, extent, spread, reach, shards=(), held_as=jnp.bfloat16):
    level = shard_levels(stream_key, extent, shards, -0.22, 0.18) if shards else 1.0
    values = jax.random.normal(stream_key, extent, jnp.float32) * spread * level
    return jnp.minimum(jnp.maximum(values, -reach), reach).astype(held_as)


def gaussian_with(key, dims, spread, most, pieces, heavy, kind=jnp.bfloat16):
    result = spread * jax.random.normal(key, dims, jnp.float32)
    if pieces:
        result = result * shard_levels(key, dims, pieces, -0.22, 0.18)
    return jnp.clip(raised(result, jax.random.fold_in(key, 3), *heavy), -most, most).astype(kind)


def setup_inputs(seed: int = 0) -> dict:
    seeds = jax.random.split(jax.random.key(seed), 12)
    x_new = scatter_about(seeds[0], (TOKENS_B, D), 1.0, 6.0, ((0, 8), (1, 64)))
    routes_new_keys = jax.random.split(jax.random.fold_in(seeds[1], 1), TOKENS_B // TOK_B)
    routes_new_turns = jax.random.permutation(jax.random.fold_in(seeds[1], 3), TOKENS_B // TOK_B)
    routes_new = jax.vmap(lambda own, number: assign_block(jax.random.fold_in(seeds[1], 2), own, number, TOK_B, EXPERTS, 2, CAP_B, 2))(routes_new_keys, routes_new_turns).reshape((TOKENS_B, 2))
    gates_new = jnp.clip(0.2 + 0.8 * jax.random.uniform(seeds[2], (TOKENS_B, 2), jnp.float32) ** shard_levels(seeds[2], (TOKENS_B, 2), ((0, 8),), -0.2, 0.2), 0.2, 1.0)
    w_gate = scatter_about(seeds[3], (EXPERTS, D, FF), D ** -0.5, 0.09375, ((0, 8), (2, 64)))
    w_up = scatter_about(seeds[4], (EXPERTS, D, FF), D ** -0.5, 0.09375, ((0, 8), (2, 64)))
    w_down = gaussian_with(seeds[5], (EXPERTS, FF, D), FF ** -0.5, 0.1875, ((0, 8), (1, 64)), (1, 2, 64, 4.0))
    grad_out = scatter_about(seeds[6], (TOKENS_A, D), 1.0, 6.0, ((0, 8), (1, 64)))
    routes_old_keys = jax.random.split(jax.random.fold_in(seeds[7], 1), TOKENS_A // TOK_A)
    routes_old_turns = jax.random.permutation(jax.random.fold_in(seeds[7], 3), TOKENS_A // TOK_A)
    routes_old = jax.vmap(lambda own, number: assign_block(jax.random.fold_in(seeds[7], 2), own, number, TOK_A, EXPERTS, 2, CAP_A, 2))(routes_old_keys, routes_old_turns).reshape((TOKENS_A, 2))
    gates_old = jnp.clip(0.2 + 0.8 * jax.random.uniform(seeds[8], (TOKENS_A, 2), jnp.float32) ** shard_levels(seeds[8], (TOKENS_A, 2), ((0, 8),), -0.2, 0.2), 0.2, 1.0)
    pre_gate = scatter_about(seeds[9], (EXPERTS, EXPERTS * CAP_A, FF), 1.5, 8.0, ((0, 8), (2, 64)))
    pre_up = scatter_about(seeds[10], (EXPERTS, EXPERTS * CAP_A, FF), 1.0, 6.0, ((0, 8), (2, 64)))
    return {"x_new": x_new, "routes_new": routes_new, "gates_new": gates_new, "w_gate": w_gate, "w_up": w_up, "w_down": w_down, "grad_out": grad_out, "routes_old": routes_old, "gates_old": gates_old, "pre_gate": pre_gate, "pre_up": pre_up}


def slot_table(routes, capacity, experts):
    pairs = routes.reshape(-1)
    onehot = (pairs[:, None] == jnp.arange(experts, dtype=jnp.int32)[None, :]).astype(jnp.int32)
    before = jnp.cumsum(onehot, axis=0) - onehot
    slot = jnp.sum(before * onehot, axis=1)
    column = pairs * capacity + slot
    table = (jnp.arange(experts * capacity, dtype=jnp.int32)[:, None] == column[None, :]).astype(jnp.float32)
    return table.reshape(experts * capacity, routes.shape[0], 2)


def to_experts(buffers, capacity):
    groups = buffers.shape[0]
    width = buffers.shape[2]
    split = buffers.reshape(groups, groups, capacity, width)
    return jnp.transpose(split, (1, 0, 2, 3)).reshape(groups, groups * capacity, width)


def reference(x_new, routes_new, gates_new, w_gate, w_up, w_down, grad_out, routes_old, gates_old, pre_gate, pre_up):
    experts = EXPERTS
    tables = jax.vmap(lambda r: slot_table(r, CAP_B, experts))(routes_new.reshape(experts, TOK_B, 2))
    picks = jnp.sum(tables, axis=3)
    grouped = x_new.reshape(experts, TOK_B, D).astype(jnp.float32)
    buffers = jnp.einsum('sct,std->scd', picks, grouped, precision=lax.Precision.HIGHEST)
    expert_in = to_experts(buffers, CAP_B).astype(jnp.bfloat16)

    def forward(items):
        rows, gate_w, up_w, down_w = items
        gate_pre = jnp.dot(rows, gate_w, preferred_element_type=jnp.float32)
        up_pre = jnp.dot(rows, up_w, preferred_element_type=jnp.float32)
        hidden = (jax.nn.silu(gate_pre) * up_pre).astype(jnp.bfloat16)
        return jnp.dot(hidden, down_w, preferred_element_type=jnp.float32).astype(jnp.bfloat16)

    expert_out = lax.map(forward, (expert_in, w_gate, w_up, w_down))
    back = to_experts(expert_out, CAP_B).astype(jnp.float32)
    weighted = jnp.sum(tables * gates_new.reshape(experts, 1, TOK_B, 2), axis=3)
    mixed = jnp.einsum('sct,scd->std', weighted, back, precision=lax.Precision.HIGHEST)
    mixed = mixed.reshape(TOKENS_B, D).astype(jnp.bfloat16)

    tables_old = jax.vmap(lambda r: slot_table(r, CAP_A, experts))(routes_old.reshape(experts, TOK_A, 2))
    weighted_old = jnp.sum(tables_old * gates_old.reshape(experts, 1, TOK_A, 2), axis=3)
    grouped_old = grad_out.reshape(experts, TOK_A, D).astype(jnp.float32)
    cot_buffers = jnp.einsum('sct,std->scd', weighted_old, grouped_old, precision=lax.Precision.HIGHEST)
    cotangent = to_experts(cot_buffers.astype(jnp.bfloat16), CAP_A)

    def backward(items):
        rows, saved_gate, saved_up, down_w = items
        gate_pre = saved_gate.astype(jnp.float32)
        up_pre = saved_up.astype(jnp.float32)
        sigma = jax.nn.sigmoid(gate_pre)
        active = gate_pre * sigma
        hidden = (active * up_pre).astype(jnp.bfloat16)
        weight_grad = jnp.dot(hidden.T, rows, preferred_element_type=jnp.float32).astype(jnp.bfloat16)
        grad_hidden = jnp.dot(rows, down_w.T, preferred_element_type=jnp.float32)
        gate_grad = (grad_hidden * up_pre * sigma * (1.0 + gate_pre * (1.0 - sigma))).astype(jnp.bfloat16)
        up_grad = (grad_hidden * active).astype(jnp.bfloat16)
        return weight_grad, gate_grad, up_grad

    grad_down, grad_gate, grad_up = lax.map(backward, (cotangent, pre_gate, pre_up, w_down))
    return mixed, grad_down, grad_gate, grad_up
```

```python
import functools

import jax
import jax.numpy as jnp
from jax import lax
from jax.experimental import pallas as pl
from jax.experimental.pallas import tpu as pltpu
from jax.sharding import Mesh
from jax.sharding import PartitionSpec as P

CAP_B = 32
CAP_A = 64
EXPERT = ("expert_0", "expert_1")
DP = ("dp_0", "dp_1", "dp_2")
Z = "dp_0"
CORE = "dp_2"
PLANE = ("dp_1", "expert_0", "expert_1")
F = 32
BF = jnp.bfloat16
F32 = jnp.float32
LAST = (((1,), (1,)), ((), ()))
MIB = 1 << 20


def iota(shape, dim):
    return lax.broadcasted_iota(jnp.int32, shape, dim)


def dot(a, b):
    return jnp.dot(a, b, preferred_element_type=F32)


def dot_last(a, b):
    return lax.dot_general(a, b, LAST, preferred_element_type=F32)


def call(body, outs, *args, flops=10**7, moved=10**6, scalars=0):
    vmem = pl.BlockSpec(memory_space=pltpu.VMEM)
    smem = pl.BlockSpec(memory_space=pltpu.SMEM)
    many = isinstance(outs, (tuple, list))
    return pl.pallas_call(
        body,
        out_shape=outs,
        in_specs=[smem] * scalars + [vmem] * (len(args) - scalars),
        out_specs=tuple(vmem for _ in outs) if many else vmem,
        cost_estimate=pl.CostEstimate(flops=flops, bytes_accessed=moved, transcendentals=0),
        compiler_params=pltpu.CompilerParams(vmem_limit_bytes=40 * MIB),
        name=body.__name__,
    )(*args)


def shape(*dims, dtype=BF):
    return jax.ShapeDtypeStruct(dims, dtype)


def lane_order(me):
    i, j = iota((512, 512), 0), iota((512, 512), 1)
    core = jnp.bitwise_xor((i // 64) % 2, me)
    hit = (
        (i // 128 == (j // F) % 4)
        & (core == j // 256)
        & ((i // F) % 2 == (j // 128) % 2)
        & (i % F == j % F)
    )
    return jnp.where(hit, 1.0, 0.0).astype(BF)


def weights_kernel(me_ref, gate_ref, up_ref, down_ref, gu_ref, dn_ref):
    order = lane_order(me_ref[0])
    gu_ref[...] = jnp.zeros_like(gu_ref)
    dn_ref[...] = jnp.zeros_like(dn_ref)
    hidden = gate_ref.shape[0]
    for ref, out, base in ((gate_ref, gu_ref, 0), (up_ref, gu_ref, 128), (down_ref, dn_ref, 0)):
        for xh in range(2):
            for zq in range(4):
                tiles = [
                    ref[:, pl.ds((zq * 4 + zi) * 256 + xh * 128, 128)] for zi in range(4)
                ]
                moved = dot(jnp.concatenate(tiles, axis=1), order).astype(BF)
                for o in range(2):
                    for h in range(2):
                        out[o, xh, pl.ds(base, hidden), pl.ds(h * 512 + zq * 128, 128)] = moved[
                            :, (o * 2 + h) * 128 : (o * 2 + h + 1) * 128
                        ]


def pack_kernel(x_ref, g_ref, out_ref):
    x = x_ref[...]
    toks, feats = x.shape
    twice = jnp.concatenate([x, x], axis=0)
    keep = iota(twice.shape, 1) // F == iota(twice.shape, 0) // toks
    twice = jnp.where(keep, twice, jnp.zeros_like(twice))
    pick = jnp.where(iota((F, feats), 1) % F == iota((F, feats), 0), 1.0, 0.0).astype(BF)
    block = jnp.concatenate([dot_last(pick, twice).astype(BF), g_ref[...]], axis=0)
    for z in range(out_ref.shape[0]):
        out_ref[z] = block


def placed(routes, rows, capacity, tokens):
    lanes = routes.shape[1]
    expert = iota((rows, lanes), 0) // capacity
    slot = iota((rows, lanes), 0) % capacity
    first, second = routes[0:1, :] == expert, routes[1:2, :] == expert
    named = first | second
    i, j = iota((lanes, lanes), 0), iota((lanes, lanes), 1)
    earlier = jnp.where((i < tokens) & (i < j % tokens), 1.0, 0.0).astype(BF)
    before = dot(jnp.where(named, 1.0, 0.0).astype(BF), earlier)
    return named & (before == slot.astype(F32)), first, second


def rows_new_kernel(routes_ref, got_ref, out_ref):
    routes = routes_ref[...]
    rows = out_ref.shape[1]
    toks = routes.shape[1] // 2
    hit, _, _ = placed(routes, rows, CAP_B, toks)
    lane = iota(hit.shape, 1) // toks
    x = got_ref[:, 0:F, :].reshape(-1, 2 * toks)
    width = x.shape[0]
    for h in range(2):
        picks = jnp.where(hit & (lane == h), 1.0, 0.0).astype(BF)
        block = dot_last(picks, x).astype(BF)
        for xh in range(2):
            out_ref[xh, :, h * width : (h + 1) * width] = block


def rows_old_kernel(routes_ref, gates_ref, got_ref, out_ref):
    routes, gates = routes_ref[...], gates_ref[...]
    rows, toks = out_ref.shape[1], routes.shape[1]
    hit, first, second = placed(routes, rows, CAP_A, toks)
    weight = jnp.where(first, gates[0:1, :], 0.0) + jnp.where(second, gates[1:2, :], 0.0)
    weight = jnp.sum(jnp.where(hit, weight, 0.0), axis=1, keepdims=True)
    picks = jnp.where(hit, 1.0, 0.0).astype(BF)
    for h in range(2):
        g = got_ref[:, F * (1 + h) : F * (2 + h), :].reshape(-1, toks)
        block = (dot_last(picks, g) * weight).astype(BF)
        width = block.shape[1]
        for xh in range(2):
            out_ref[xh, :, h * width : (h + 1) * width] = block


def up_kernel(own_ref, other_ref, gu_ref, dn_ref, hidden_ref, out_ref):
    total = None
    for o, ref in enumerate((own_ref, other_ref)):
        for xh in range(2):
            term = dot_last(ref[xh], gu_ref[o, xh])
            total = term if total is None else total + term
    gate, up = total[:, :128], total[:, 128:]
    hidden = (gate / (1.0 + jnp.exp(-gate)) * up).astype(BF)
    hidden_ref[...] = hidden
    for xh in range(2):
        out_ref[xh] = dot(hidden, dn_ref[1, xh]).astype(BF)


def down_kernel(hidden_ref, dn_ref, arrived_ref, out_ref):
    hidden = hidden_ref[...]
    for xh in range(2):
        out_ref[xh] = (dot(hidden, dn_ref[0, xh]) + arrived_ref[xh].astype(F32)).astype(BF)


def mix_kernel(routes_ref, gates_ref, got_ref, out_ref):
    routes, gates = routes_ref[...], gates_ref[...]
    rows, width = got_ref.shape[1], got_ref.shape[2] // 2
    toks = routes.shape[1] // 2
    hit, first, second = placed(routes, rows, CAP_B, toks)
    weight = jnp.where(first, gates[0:1, :], 0.0) + jnp.where(second, gates[1:2, :], 0.0)
    weight = jnp.where(hit, weight, 0.0).T[:toks]
    high = weight.astype(BF)
    rest = weight - high.astype(F32)
    middle = rest.astype(BF)
    low = (rest - middle.astype(F32)).astype(BF)
    halves = []
    for h in range(2):
        total = None
        for xh in range(2):
            got = got_ref[xh, :, h * width : (h + 1) * width]
            for part in (high, middle, low):
                term = dot(part, got)
                total = term if total is None else total + term
        halves.append(total)
    mixed = jnp.concatenate(halves, axis=0).T.astype(BF)
    out_ref[...] = mixed.reshape(out_ref.shape)


def total_kernel(got_ref, out_ref):
    total = got_ref[0].astype(F32)
    for z in range(1, got_ref.shape[0]):
        total = total + got_ref[z].astype(F32)
    turned = total.T
    toks = out_ref.shape[0]
    out_ref[...] = jnp.concatenate([turned[:toks], turned[toks:]], axis=1).astype(BF)


def back_kernel(me_ref, own_ref, other_ref, dn_ref, gate_ref, up_ref, down_ref, dg_ref, du_ref, held):
    total = None
    refs = (own_ref, other_ref)
    for o, ref in enumerate(refs):
        for xh in range(2):
            term = dot_last(dn_ref[o, xh], ref[xh])
            total = term if total is None else total + term
    gate, up = gate_ref[...].astype(F32), up_ref[...].astype(F32)
    grad = total[: gate.shape[0]]
    sigma = 1.0 / (1.0 + jnp.exp(-gate))
    active = gate * sigma
    dg_ref[...] = (grad * up * sigma * (1.0 + gate * (1.0 - sigma))).astype(BF)
    du_ref[...] = (grad * active).astype(BF)
    hidden = (active * up).astype(BF)
    for o, ref in enumerate(refs):
        for xh in range(2):
            held[o, xh] = dot(hidden, ref[xh]).astype(BF)
    order = lane_order(me_ref[0])
    for xh in range(2):
        for zq in range(4):
            tiles = [
                held[o, xh, :, pl.ds(h * 512 + zq * 128, 128)] for o in range(2) for h in range(2)
            ]
            moved = dot_last(jnp.concatenate(tiles, axis=1), order).astype(BF)
            for zi in range(4):
                down_ref[:, pl.ds((zq * 4 + zi) * 256 + xh * 128, 128)] = moved[
                    :, zi * 128 : (zi + 1) * 128
                ]


def other_core(array):
    return lax.ppermute(array, CORE, [(0, 1), (1, 0)])


def over_plane(rows):
    peers = rows.reshape(16, -1, rows.shape[2])
    return lax.all_to_all(peers, PLANE, 0, 0, tiled=True).reshape(rows.shape)


def per_device(
    x_new,
    routes_new,
    gates_new,
    w_gate,
    w_up,
    w_down,
    grad_out,
    routes_old,
    gates_old,
    pre_gate,
    pre_up,
):
    me = lax.axis_index(CORE).astype(jnp.int32).reshape(1)
    experts = lax.axis_size(EXPERT)
    rows_new, rows_old = experts * CAP_B, experts * CAP_A
    hidden_units = w_gate.shape[2]
    twice = lambda a: jnp.concatenate([a.T, a.T], axis=1)
    routes_b, gates_b = twice(routes_new), twice(gates_new)
    routes_a, gates_a = routes_old.T, gates_old.T

    packed = call(pack_kernel, shape(16, 3 * F, 128), x_new, grad_out.T)
    got = lax.all_to_all(packed, Z, 0, 0, tiled=True)
    gate_up, down = call(
        weights_kernel,
        (shape(2, 2, 256, 1024), shape(2, 2, 128, 1024)),
        me,
        w_gate[0].T,
        w_up[0].T,
        w_down[0],
        scalars=1,
        flops=14 * 10**8,
        moved=6 * 10**6,
    )

    own = over_plane(call(rows_new_kernel, shape(2, rows_new, 1024), routes_b, got))
    other = other_core(own)
    hidden, partial = call(
        up_kernel,
        (shape(rows_new, 128), shape(2, rows_new, 1024)),
        own,
        other,
        gate_up,
        down,
        flops=8 * 10**8,
        moved=4 * 10**6,
    )
    summed = call(
        down_kernel, shape(2, rows_new, 1024), hidden, down, other_core(partial), flops=2 * 10**8
    )
    mixed = call(
        mix_kernel, shape(16, F, 128), routes_b, gates_b, over_plane(summed), flops=4 * 10**8
    )
    mixed = lax.all_to_all(mixed, Z, 0, 0, tiled=True)
    mixed = call(total_kernel, shape(*x_new.shape), mixed)

    own_a = over_plane(call(rows_old_kernel, shape(2, rows_old, 1024), routes_a, gates_a, got))
    other_a = other_core(own_a)
    vmem = pl.BlockSpec(memory_space=pltpu.VMEM)
    weight_grad, gate_grad, up_grad = pl.pallas_call(
        back_kernel,
        out_shape=(
            shape(hidden_units, 4096),
            shape(hidden_units, rows_old),
            shape(hidden_units, rows_old),
        ),
        in_specs=[pl.BlockSpec(memory_space=pltpu.SMEM)] + [vmem] * 5,
        out_specs=(vmem,) * 3,
        scratch_shapes=[pltpu.VMEM((2, 2, hidden_units, 1024), BF)],
        cost_estimate=pl.CostEstimate(
            flops=15 * 10**8, bytes_accessed=8 * 10**6, transcendentals=0
        ),
        compiler_params=pltpu.CompilerParams(vmem_limit_bytes=40 * MIB),
        name="back_kernel",
    )(me, own_a, other_a, down, pre_gate[0].T, pre_up[0].T)
    return (mixed, weight_grad[None], gate_grad.T[None], up_grad.T[None])


def solution(mesh):
    torus = Mesh(
        mesh.devices.reshape(4, 2, 16, 2, 2), ("expert_0", "expert_1", "dp_0", "dp_1", "dp_2")
    )
    placed_as = (
        P(EXPERT, DP),
        P(EXPERT, None),
        P(EXPERT, None),
        P(EXPERT, None, DP),
        P(EXPERT, None, DP),
        P(EXPERT, DP, None),
        P(EXPERT, DP),
        P(EXPERT, None),
        P(EXPERT, None),
        P(EXPERT, None, DP),
        P(EXPERT, None, DP),
    )
    return jax.shard_map(
        per_device,
        mesh=torus,
        in_specs=placed_as,
        out_specs=(P(EXPERT, DP), P(EXPERT, DP, None), P(EXPERT, None, DP), P(EXPERT, None, DP)),
        check_vma=False,
    )
```

```python
import functools

import jax
import jax.numpy as jnp
from jax import lax
from jax.experimental import pallas as pl
from jax.experimental.pallas import tpu as pltpu
from jax.sharding import Mesh
from jax.sharding import PartitionSpec as P

CAP_B = 32
CAP_A = 64
EXPERT = ("expert_0", "expert_1")
DP = ("dp_0", "dp_1", "dp_2")
Z = "dp_0"
CORE = "dp_2"
XH = "dp_1"
PLANE = ("dp_1", "expert_0", "expert_1")
F = 32
BF = jnp.bfloat16
F32 = jnp.float32
LAST = (((1,), (1,)), ((), ()))
MIB = 1 << 20


def iota(shape, dim):
    return lax.broadcasted_iota(jnp.int32, shape, dim)


def dot(a, b):
    return jnp.dot(a, b, preferred_element_type=F32)


def dot_last(a, b):
    return lax.dot_general(a, b, LAST, preferred_element_type=F32)


def call(body, outs, *args, flops=10**7, moved=10**6, scalars=0):
    vmem = pl.BlockSpec(memory_space=pltpu.VMEM)
    smem = pl.BlockSpec(memory_space=pltpu.SMEM)
    many = isinstance(outs, (tuple, list))
    return pl.pallas_call(
        body,
        out_shape=outs,
        in_specs=[smem] * scalars + [vmem] * (len(args) - scalars),
        out_specs=tuple(vmem for _ in outs) if many else vmem,
        cost_estimate=pl.CostEstimate(flops=flops, bytes_accessed=moved, transcendentals=0),
        compiler_params=pltpu.CompilerParams(vmem_limit_bytes=16 * MIB),
        name=body.__name__,
    )(*args)


def shape(*dims, dtype=BF):
    return jax.ShapeDtypeStruct(dims, dtype)


def lane_order(me):
    i, j = iota((512, 512), 0), iota((512, 512), 1)
    core = jnp.bitwise_xor((i // 64) % 2, me)
    hit = (
        (i // 128 == (j // F) % 4)
        & (core == j // 256)
        & ((i // F) % 2 == (j // 128) % 2)
        & (i % F == j % F)
    )
    return jnp.where(hit, 1.0, 0.0).astype(BF)


def weights_kernel(me_ref, gate_ref, up_ref, down_ref, gu_ref, dn_ref):
    order = lane_order(me_ref[0])
    gu_ref[...] = jnp.zeros_like(gu_ref)
    dn_ref[...] = jnp.zeros_like(dn_ref)
    hidden = gate_ref.shape[0]
    for ref, out, base in ((gate_ref, gu_ref, 0), (up_ref, gu_ref, 128), (down_ref, dn_ref, 0)):
        for xh in range(2):
            for zq in range(4):
                tiles = [
                    ref[:, pl.ds((zq * 4 + zi) * 256 + xh * 128, 128)] for zi in range(4)
                ]
                moved = dot(jnp.concatenate(tiles, axis=1), order).astype(BF)
                for o in range(2):
                    for h in range(2):
                        out[o, xh, pl.ds(base, hidden), pl.ds(h * 512 + zq * 128, 128)] = moved[
                            :, (o * 2 + h) * 128 : (o * 2 + h + 1) * 128
                        ]


def pack_kernel(x_ref, g_ref, out_ref):
    x = x_ref[...]
    toks, feats = x.shape
    twice = jnp.concatenate([x, x], axis=0)
    keep = iota(twice.shape, 1) // F == iota(twice.shape, 0) // toks
    twice = jnp.where(keep, twice, jnp.zeros_like(twice))
    pick = jnp.where(iota((F, feats), 1) % F == iota((F, feats), 0), 1.0, 0.0).astype(BF)
    block = jnp.concatenate([dot_last(pick, twice).astype(BF), g_ref[...]], axis=0)
    for z in range(out_ref.shape[0]):
        out_ref[z] = block


def placed(routes, rows, capacity, tokens):
    lanes = routes.shape[1]
    expert = iota((rows, lanes), 0) // capacity
    slot = iota((rows, lanes), 0) % capacity
    first, second = routes[0:1, :] == expert, routes[1:2, :] == expert
    named = first | second
    i, j = iota((lanes, lanes), 0), iota((lanes, lanes), 1)
    earlier = jnp.where((i < tokens) & (i < j % tokens), 1.0, 0.0).astype(BF)
    before = dot(jnp.where(named, 1.0, 0.0).astype(BF), earlier)
    return named & (before == slot.astype(F32)), first, second


def rows_new_kernel(routes_ref, got_ref, out_ref):
    routes = routes_ref[...]
    rows = out_ref.shape[1]
    toks = routes.shape[1] // 2
    hit, _, _ = placed(routes, rows, CAP_B, toks)
    lane = iota(hit.shape, 1) // toks
    x = got_ref[:, 0:F, :].reshape(-1, 2 * toks)
    width = x.shape[0]
    for h in range(2):
        picks = jnp.where(hit & (lane == h), 1.0, 0.0).astype(BF)
        block = dot_last(picks, x).astype(BF)
        for xh in range(2):
            out_ref[xh, :, h * width : (h + 1) * width] = block


def rows_old_kernel(me_ref, routes_ref, gates_ref, got_ref, other_ref, out_ref):
    routes, gates = routes_ref[...], gates_ref[...]
    experts, _, slots, width = out_ref.shape
    toks = routes.shape[1]
    hit, first, second = placed(routes, experts * slots, slots, toks)
    weight = jnp.where(first, gates[0:1, :], 0.0) + jnp.where(second, gates[1:2, :], 0.0)
    weight = jnp.sum(jnp.where(hit, weight, 0.0), axis=1, keepdims=True)
    picks = jnp.where(hit, 1.0, 0.0).astype(BF)
    mine = me_ref[1]
    for xh, ref, base in ((mine, got_ref, F), (1 - mine, other_ref, 0)):
        for h in range(2):
            g = ref[:, base + F * h : base + F * (1 + h), :].reshape(-1, toks)
            block = (dot_last(picks, g) * weight).astype(BF).reshape(experts, slots, -1)
            out_ref[:, xh, :, h * (width // 2) : (h + 1) * (width // 2)] = block


def up_kernel(own_ref, other_ref, gu_ref, dn_ref, hidden_ref, out_ref):
    total = None
    for o, ref in enumerate((own_ref, other_ref)):
        for xh in range(2):
            term = dot_last(ref[xh], gu_ref[o, xh])
            total = term if total is None else total + term
    gate, up = total[:, :128], total[:, 128:]
    hidden = (gate / (1.0 + jnp.exp(-gate)) * up).astype(BF)
    hidden_ref[...] = hidden
    for xh in range(2):
        out_ref[xh] = dot(hidden, dn_ref[1, xh]).astype(BF)


def down_kernel(hidden_ref, dn_ref, arrived_ref, out_ref):
    hidden = hidden_ref[...]
    for xh in range(2):
        out_ref[xh] = (dot(hidden, dn_ref[0, xh]) + arrived_ref[xh].astype(F32)).astype(BF)


def mix_kernel(routes_ref, gates_ref, got_ref, out_ref):
    routes, gates = routes_ref[...], gates_ref[...]
    rows, width = got_ref.shape[1], got_ref.shape[2] // 2
    toks = routes.shape[1] // 2
    hit, first, second = placed(routes, rows, CAP_B, toks)
    weight = jnp.where(first, gates[0:1, :], 0.0) + jnp.where(second, gates[1:2, :], 0.0)
    weight = jnp.where(hit, weight, 0.0).T[:toks]
    high = weight.astype(BF)
    rest = weight - high.astype(F32)
    middle = rest.astype(BF)
    low = (rest - middle.astype(F32)).astype(BF)
    halves = []
    for h in range(2):
        total = None
        for xh in range(2):
            got = got_ref[xh, :, h * width : (h + 1) * width]
            for part in (high, middle, low):
                term = dot(part, got)
                total = term if total is None else total + term
        halves.append(total)
    mixed = jnp.concatenate(halves, axis=0).T.astype(BF)
    out_ref[...] = mixed.reshape(out_ref.shape)


def total_kernel(got_ref, out_ref):
    total = got_ref[0].astype(F32)
    for z in range(1, got_ref.shape[0]):
        total = total + got_ref[z].astype(F32)
    turned = total.T
    toks = out_ref.shape[0]
    out_ref[...] = jnp.concatenate([turned[:toks], turned[toks:]], axis=1).astype(BF)


def rows_of(ref, xh):
    return ref[:, xh].reshape(-1, ref.shape[3])


def back_kernel(me_ref, own_ref, other_ref, dn_ref, gate_ref, up_ref, down_ref, dg_ref, du_ref, held):
    total = None
    refs = (own_ref, other_ref)
    for o, ref in enumerate(refs):
        for xh in range(2):
            term = dot_last(dn_ref[o, xh], rows_of(ref, xh))
            total = term if total is None else total + term
    gate, up = gate_ref[...].astype(F32), up_ref[...].astype(F32)
    grad = total[: gate.shape[0]]
    sigma = 1.0 / (1.0 + jnp.exp(-gate))
    active = gate * sigma
    dg_ref[...] = (grad * up * sigma * (1.0 + gate * (1.0 - sigma))).astype(BF)
    du_ref[...] = (grad * active).astype(BF)
    hidden = (active * up).astype(BF)
    for o, ref in enumerate(refs):
        for xh in range(2):
            held[o, xh] = dot(hidden, rows_of(ref, xh)).astype(BF)
    order = lane_order(me_ref[0])
    for xh in range(2):
        for zq in range(4):
            tiles = [
                held[o, xh, :, pl.ds(h * 512 + zq * 128, 128)] for o in range(2) for h in range(2)
            ]
            moved = dot_last(jnp.concatenate(tiles, axis=1), order).astype(BF)
            for zi in range(4):
                down_ref[:, pl.ds((zq * 4 + zi) * 256 + xh * 128, 128)] = moved[
                    :, zi * 128 : (zi + 1) * 128
                ]


def other_core(array):
    return lax.ppermute(array, CORE, [(0, 1), (1, 0)])


def over_plane(rows):
    peers = rows.reshape(16, -1, rows.shape[2])
    return lax.all_to_all(peers, PLANE, 0, 0, tiled=True).reshape(rows.shape)


def per_device(
    x_new,
    routes_new,
    gates_new,
    w_gate,
    w_up,
    w_down,
    grad_out,
    routes_old,
    gates_old,
    pre_gate,
    pre_up,
):
    me = jnp.stack([lax.axis_index(CORE), lax.axis_index(XH)]).astype(jnp.int32)
    experts = lax.axis_size(EXPERT)
    rows_new, rows_old = experts * CAP_B, experts * CAP_A
    hidden_units = w_gate.shape[2]
    twice = lambda a: jnp.concatenate([a.T, a.T], axis=1)
    routes_b, gates_b = twice(routes_new), twice(gates_new)
    routes_a, gates_a = routes_old.T, gates_old.T

    packed = call(pack_kernel, shape(16, 3 * F, 128), x_new, grad_out.T)
    got = lax.all_to_all(packed, Z, 0, 0, tiled=True)
    gate_up, down = call(
        weights_kernel,
        (shape(2, 2, 256, 1024), shape(2, 2, 128, 1024)),
        me,
        w_gate[0].T,
        w_up[0].T,
        w_down[0],
        scalars=1,
        flops=14 * 10**8,
        moved=6 * 10**6,
    )

    got, gate_up, down = lax.optimization_barrier((got, gate_up, down))

    own = over_plane(call(rows_new_kernel, shape(2, rows_new, 1024), routes_b, got))
    other = other_core(own)
    hidden, partial = call(
        up_kernel,
        (shape(rows_new, 128), shape(2, rows_new, 1024)),
        own,
        other,
        gate_up,
        down,
        flops=8 * 10**8,
        moved=4 * 10**6,
    )
    summed = call(
        down_kernel, shape(2, rows_new, 1024), hidden, down, other_core(partial), flops=2 * 10**8
    )
    mixed = call(
        mix_kernel, shape(16, F, 128), routes_b, gates_b, over_plane(summed), flops=4 * 10**8
    )
    mixed = lax.all_to_all(mixed, Z, 0, 0, tiled=True)
    mixed = call(total_kernel, shape(*x_new.shape), mixed)

    far = lax.ppermute(got[:, F:], XH, [(0, 1), (1, 0)])
    rows_a = call(
        rows_old_kernel,
        shape(experts, 2, CAP_A, 1024),
        me,
        routes_a,
        gates_a,
        got,
        far,
        scalars=1,
    )
    own_a = lax.all_to_all(rows_a, EXPERT, 0, 0, tiled=True)
    other_a = other_core(own_a)
    vmem = pl.BlockSpec(memory_space=pltpu.VMEM)
    weight_grad, gate_grad, up_grad = pl.pallas_call(
        back_kernel,
        out_shape=(
            shape(hidden_units, 4096),
            shape(hidden_units, rows_old),
            shape(hidden_units, rows_old),
        ),
        in_specs=[pl.BlockSpec(memory_space=pltpu.SMEM)] + [vmem] * 5,
        out_specs=(vmem,) * 3,
        scratch_shapes=[pltpu.VMEM((2, 2, hidden_units, 1024), BF)],
        cost_estimate=pl.CostEstimate(
            flops=15 * 10**8, bytes_accessed=8 * 10**6, transcendentals=0
        ),
        compiler_params=pltpu.CompilerParams(vmem_limit_bytes=16 * MIB),
        name="back_kernel",
    )(me, own_a, other_a, down, pre_gate[0].T, pre_up[0].T)
    return (mixed, weight_grad[None], gate_grad.T[None], up_grad.T[None])


def solution(mesh):
    torus = Mesh(
        mesh.devices.reshape(4, 2, 16, 2, 2), ("expert_0", "expert_1", "dp_0", "dp_1", "dp_2")
    )
    placed_as = (
        P(EXPERT, DP),
        P(EXPERT, None),
        P(EXPERT, None),
        P(EXPERT, None, DP),
        P(EXPERT, None, DP),
        P(EXPERT, DP, None),
        P(EXPERT, DP),
        P(EXPERT, None),
        P(EXPERT, None),
        P(EXPERT, None, DP),
        P(EXPERT, None, DP),
    )
    return jax.shard_map(
        per_device,
        mesh=torus,
        in_specs=placed_as,
        out_specs=(P(EXPERT, DP), P(EXPERT, DP, None), P(EXPERT, None, DP), P(EXPERT, None, DP)),
        check_vma=False,
    )
```

```python
import functools

import jax
import jax.numpy as jnp
from jax import lax
from jax.experimental import pallas as pl
from jax.experimental.pallas import tpu as pltpu
from jax.sharding import Mesh
from jax.sharding import PartitionSpec as P

CAP_B = 32
CAP_A = 64
EXPERT = ("expert_0", "expert_1")
DP = ("dp_0", "dp_1", "dp_2")
Z = "dp_0"
CORE = "dp_2"
XH = "dp_1"
PLANE = ("dp_1", "expert_0", "expert_1")
F = 32
BF = jnp.bfloat16
F32 = jnp.float32
LAST = (((1,), (1,)), ((), ()))
MIB = 1 << 20


def iota(shape, dim):
    return lax.broadcasted_iota(jnp.int32, shape, dim)


def dot(a, b):
    return jnp.dot(a, b, preferred_element_type=F32)


def dot_last(a, b):
    return lax.dot_general(a, b, LAST, preferred_element_type=F32)


def call(body, outs, *args, flops=10**7, moved=10**6, scalars=0):
    vmem = pl.BlockSpec(memory_space=pltpu.VMEM)
    smem = pl.BlockSpec(memory_space=pltpu.SMEM)
    many = isinstance(outs, (tuple, list))
    return pl.pallas_call(
        body,
        out_shape=outs,
        in_specs=[smem] * scalars + [vmem] * (len(args) - scalars),
        out_specs=tuple(vmem for _ in outs) if many else vmem,
        cost_estimate=pl.CostEstimate(flops=flops, bytes_accessed=moved, transcendentals=0),
        compiler_params=pltpu.CompilerParams(vmem_limit_bytes=16 * MIB),
        name=body.__name__,
    )(*args)


def shape(*dims, dtype=BF):
    return jax.ShapeDtypeStruct(dims, dtype)


def lane_order(me):
    i, j = iota((512, 512), 0), iota((512, 512), 1)
    core = jnp.bitwise_xor((i // 64) % 2, me)
    hit = (
        (i // 128 == (j // F) % 4)
        & (core == j // 256)
        & ((i // F) % 2 == (j // 128) % 2)
        & (i % F == j % F)
    )
    return jnp.where(hit, 1.0, 0.0).astype(BF)


def weights_kernel(me_ref, gate_ref, up_ref, down_ref, gu_ref, dn_ref):
    order = lane_order(me_ref[0])
    gu_ref[...] = jnp.zeros_like(gu_ref)
    dn_ref[...] = jnp.zeros_like(dn_ref)
    hidden = gate_ref.shape[0]
    for ref, out, base in ((gate_ref, gu_ref, 0), (up_ref, gu_ref, 128), (down_ref, dn_ref, 0)):
        for xh in range(2):
            for zq in range(4):
                tiles = [
                    ref[:, pl.ds((zq * 4 + zi) * 256 + xh * 128, 128)] for zi in range(4)
                ]
                moved = dot(jnp.concatenate(tiles, axis=1), order).astype(BF)
                for o in range(2):
                    for h in range(2):
                        out[o, xh, pl.ds(base, hidden), pl.ds(h * 512 + zq * 128, 128)] = moved[
                            :, (o * 2 + h) * 128 : (o * 2 + h + 1) * 128
                        ]


def pack_kernel(x_ref, g_ref, out_ref):
    x = x_ref[...]
    toks, feats = x.shape
    twice = jnp.concatenate([x, x], axis=0)
    keep = iota(twice.shape, 1) // F == iota(twice.shape, 0) // toks
    twice = jnp.where(keep, twice, jnp.zeros_like(twice))
    pick = jnp.where(iota((F, feats), 1) % F == iota((F, feats), 0), 1.0, 0.0).astype(BF)
    block = jnp.concatenate([dot_last(pick, twice).astype(BF), g_ref[...]], axis=0)
    for z in range(out_ref.shape[0]):
        out_ref[z] = block


def placed(routes, rows, capacity, tokens):
    lanes = routes.shape[1]
    expert = iota((rows, lanes), 0) // capacity
    slot = iota((rows, lanes), 0) % capacity
    first, second = routes[0:1, :] == expert, routes[1:2, :] == expert
    named = first | second
    i, j = iota((lanes, lanes), 0), iota((lanes, lanes), 1)
    earlier = jnp.where((i < tokens) & (i < j % tokens), 1.0, 0.0).astype(BF)
    before = dot(jnp.where(named, 1.0, 0.0).astype(BF), earlier)
    return named & (before == slot.astype(F32)), first, second


def rows_new_kernel(routes_ref, got_ref, out_ref):
    routes = routes_ref[...]
    rows = out_ref.shape[1]
    toks = routes.shape[1] // 2
    hit, _, _ = placed(routes, rows, CAP_B, toks)
    lane = iota(hit.shape, 1) // toks
    x = got_ref[:, 0:F, :].reshape(-1, 2 * toks)
    width = x.shape[0]
    for h in range(2):
        picks = jnp.where(hit & (lane == h), 1.0, 0.0).astype(BF)
        block = dot_last(picks, x).astype(BF)
        for xh in range(2):
            out_ref[xh, :, h * width : (h + 1) * width] = block


def rows_old_kernel(routes_ref, gates_ref, got_ref, out_ref):
    routes, gates = routes_ref[...], gates_ref[...]
    experts, slots, width = out_ref.shape
    toks = routes.shape[1]
    hit, first, second = placed(routes, experts * slots, slots, toks)
    weight = jnp.where(first, gates[0:1, :], 0.0) + jnp.where(second, gates[1:2, :], 0.0)
    weight = jnp.sum(jnp.where(hit, weight, 0.0), axis=1, keepdims=True)
    picks = jnp.where(hit, 1.0, 0.0).astype(BF)
    for h in range(2):
        g = got_ref[:, F * (1 + h) : F * (2 + h), :].reshape(-1, toks)
        block = (dot_last(picks, g) * weight).astype(BF).reshape(experts, slots, -1)
        out_ref[:, :, h * (width // 2) : (h + 1) * (width // 2)] = block


def own_up_kernel(own_ref, gu_ref, out_ref):
    out_ref[...] = dot_last(own_ref[0], gu_ref[0, 0]) + dot_last(own_ref[1], gu_ref[0, 1])


def up_kernel(begun_ref, other_ref, gu_ref, dn_ref, hidden_ref, out_ref):
    total = begun_ref[...]
    for xh in range(2):
        total = total + dot_last(other_ref[xh], gu_ref[1, xh])
    gate, up = total[:, :128], total[:, 128:]
    hidden = (gate / (1.0 + jnp.exp(-gate)) * up).astype(BF)
    hidden_ref[...] = hidden
    for xh in range(2):
        out_ref[xh] = dot(hidden, dn_ref[1, xh]).astype(BF)


def down_kernel(hidden_ref, dn_ref, arrived_ref, out_ref):
    hidden = hidden_ref[...]
    for xh in range(2):
        out_ref[xh] = (dot(hidden, dn_ref[0, xh]) + arrived_ref[xh].astype(F32)).astype(BF)


def mix_kernel(routes_ref, gates_ref, got_ref, out_ref):
    routes, gates = routes_ref[...], gates_ref[...]
    rows, width = got_ref.shape[1], got_ref.shape[2] // 2
    toks = routes.shape[1] // 2
    hit, first, second = placed(routes, rows, CAP_B, toks)
    weight = jnp.where(first, gates[0:1, :], 0.0) + jnp.where(second, gates[1:2, :], 0.0)
    weight = jnp.where(hit, weight, 0.0).T[:toks]
    high = weight.astype(BF)
    rest = weight - high.astype(F32)
    middle = rest.astype(BF)
    low = (rest - middle.astype(F32)).astype(BF)
    halves = []
    for h in range(2):
        total = None
        for xh in range(2):
            got = got_ref[xh, :, h * width : (h + 1) * width]
            for part in (high, middle, low):
                term = dot(part, got)
                total = term if total is None else total + term
        halves.append(total)
    mixed = jnp.concatenate(halves, axis=0).T.astype(BF)
    out_ref[...] = mixed.reshape(out_ref.shape)


def total_kernel(got_ref, out_ref):
    total = got_ref[0].astype(F32)
    for z in range(1, got_ref.shape[0]):
        total = total + got_ref[z].astype(F32)
    turned = total.T
    toks = out_ref.shape[0]
    out_ref[...] = jnp.concatenate([turned[:toks], turned[toks:]], axis=1).astype(BF)


def back_kernel(
    me_ref, own_ref, far_ref, own_other_ref, far_other_ref, dn_ref, gate_ref, up_ref,
    down_ref, dg_ref, du_ref, held,
):
    mine = me_ref[1]
    parts = (
        (0, mine, own_ref),
        (1, mine, own_other_ref),
        (0, 1 - mine, far_ref),
        (1, 1 - mine, far_other_ref),
    )
    rows = lambda ref: ref[...].reshape(-1, ref.shape[2])
    total = None
    for o, xh, ref in parts:
        term = dot_last(dn_ref[o, xh], rows(ref))
        total = term if total is None else total + term
    gate, up = gate_ref[...].astype(F32), up_ref[...].astype(F32)
    grad = total[: gate.shape[0]]
    sigma = 1.0 / (1.0 + jnp.exp(-gate))
    active = gate * sigma
    dg_ref[...] = (grad * up * sigma * (1.0 + gate * (1.0 - sigma))).astype(BF)
    du_ref[...] = (grad * active).astype(BF)
    hidden = (active * up).astype(BF)
    for o, xh, ref in parts:
        held[o, xh] = dot(hidden, rows(ref)).astype(BF)
    order = lane_order(me_ref[0])
    for xh in range(2):
        for zq in range(4):
            tiles = [
                held[o, xh, :, pl.ds(h * 512 + zq * 128, 128)] for o in range(2) for h in range(2)
            ]
            moved = dot_last(jnp.concatenate(tiles, axis=1), order).astype(BF)
            for zi in range(4):
                down_ref[:, pl.ds((zq * 4 + zi) * 256 + xh * 128, 128)] = moved[
                    :, zi * 128 : (zi + 1) * 128
                ]


def other_core(array):
    return lax.ppermute(array, CORE, [(0, 1), (1, 0)])


def over_plane(rows):
    peers = rows.reshape(16, -1, rows.shape[2])
    return lax.all_to_all(peers, PLANE, 0, 0, tiled=True).reshape(rows.shape)


def per_device(
    x_new,
    routes_new,
    gates_new,
    w_gate,
    w_up,
    w_down,
    grad_out,
    routes_old,
    gates_old,
    pre_gate,
    pre_up,
):
    me = jnp.stack([lax.axis_index(CORE), lax.axis_index(XH)]).astype(jnp.int32)
    experts = lax.axis_size(EXPERT)
    rows_new, rows_old = experts * CAP_B, experts * CAP_A
    hidden_units = w_gate.shape[2]
    twice = lambda a: jnp.concatenate([a.T, a.T], axis=1)
    routes_b, gates_b = twice(routes_new), twice(gates_new)
    routes_a, gates_a = routes_old.T, gates_old.T

    packed = call(pack_kernel, shape(16, 3 * F, 128), x_new, grad_out.T)
    got = lax.all_to_all(packed, Z, 0, 0, tiled=True)
    gate_up, down = call(
        weights_kernel,
        (shape(2, 2, 256, 1024), shape(2, 2, 128, 1024)),
        me,
        w_gate[0].T,
        w_up[0].T,
        w_down[0],
        scalars=1,
        flops=14 * 10**8,
        moved=6 * 10**6,
    )

    got, gate_up, down = lax.optimization_barrier((got, gate_up, down))

    own = over_plane(call(rows_new_kernel, shape(2, rows_new, 1024), routes_b, got))
    rows_a = call(rows_old_kernel, shape(experts, CAP_A, 1024), routes_a, gates_a, got)
    own, rows_a = lax.optimization_barrier((own, rows_a))
    other = other_core(own)
    begun = call(own_up_kernel, shape(rows_new, 256, dtype=F32), own, gate_up, flops=3 * 10**8)
    hidden, partial = call(
        up_kernel,
        (shape(rows_new, 128), shape(2, rows_new, 1024)),
        begun,
        other,
        gate_up,
        down,
        flops=8 * 10**8,
        moved=4 * 10**6,
    )
    summed = call(
        down_kernel, shape(2, rows_new, 1024), hidden, down, other_core(partial), flops=2 * 10**8
    )
    mixed = call(
        mix_kernel, shape(16, F, 128), routes_b, gates_b, over_plane(summed), flops=4 * 10**8
    )
    mixed = lax.all_to_all(mixed, Z, 0, 0, tiled=True)
    mixed = call(total_kernel, shape(*x_new.shape), mixed)

    own_a = lax.all_to_all(rows_a, EXPERT, 0, 0, tiled=True)
    far_a = lax.ppermute(own_a, XH, [(0, 1), (1, 0)])
    own_other, far_other = other_core(own_a), other_core(far_a)
    vmem = pl.BlockSpec(memory_space=pltpu.VMEM)
    weight_grad, gate_grad, up_grad = pl.pallas_call(
        back_kernel,
        out_shape=(
            shape(hidden_units, 4096),
            shape(hidden_units, rows_old),
            shape(hidden_units, rows_old),
        ),
        in_specs=[pl.BlockSpec(memory_space=pltpu.SMEM)] + [vmem] * 7,
        out_specs=(vmem,) * 3,
        scratch_shapes=[pltpu.VMEM((2, 2, hidden_units, 1024), BF)],
        cost_estimate=pl.CostEstimate(
            flops=15 * 10**8, bytes_accessed=8 * 10**6, transcendentals=0
        ),
        compiler_params=pltpu.CompilerParams(vmem_limit_bytes=16 * MIB),
        name="back_kernel",
    )(me, own_a, far_a, own_other, far_other, down, pre_gate[0].T, pre_up[0].T)
    return (mixed, weight_grad[None], gate_grad.T[None], up_grad.T[None])


def solution(mesh):
    torus = Mesh(
        mesh.devices.reshape(4, 2, 16, 2, 2), ("expert_0", "expert_1", "dp_0", "dp_1", "dp_2")
    )
    placed_as = (
        P(EXPERT, DP),
        P(EXPERT, None),
        P(EXPERT, None),
        P(EXPERT, None, DP),
        P(EXPERT, None, DP),
        P(EXPERT, DP, None),
        P(EXPERT, DP),
        P(EXPERT, None),
        P(EXPERT, None),
        P(EXPERT, None, DP),
        P(EXPERT, None, DP),
    )
    return jax.shard_map(
        per_device,
        mesh=torus,
        in_specs=placed_as,
        out_specs=(P(EXPERT, DP), P(EXPERT, DP, None), P(EXPERT, None, DP), P(EXPERT, None, DP)),
        check_vma=False,
    )
```

```python
import functools

import jax
import jax.numpy as jnp
from jax import lax
from jax.experimental import pallas as pl
from jax.experimental.pallas import tpu as pltpu
from jax.sharding import Mesh
from jax.sharding import PartitionSpec as P

CAP_B = 32
CAP_A = 64
EXPERT = ("expert_0", "expert_1")
DP = ("dp_0", "dp_1", "dp_2")
Z = "dp_0"
CORE = "dp_2"
XH = "dp_1"
PLANE = ("expert_0", "expert_1", "dp_1")
Z_XH = ("dp_0", "dp_1")
F = 32
BF = jnp.bfloat16
F32 = jnp.float32
LAST = (((1,), (1,)), ((), ()))
MIB = 1 << 20


def iota(shape, dim):
    return lax.broadcasted_iota(jnp.int32, shape, dim)


def dot(a, b):
    return jnp.dot(a, b, preferred_element_type=F32)


def dot_last(a, b):
    return lax.dot_general(a, b, LAST, preferred_element_type=F32)


def call(body, outs, *args, flops=10**7, moved=10**6, scalars=0):
    vmem = pl.BlockSpec(memory_space=pltpu.VMEM)
    smem = pl.BlockSpec(memory_space=pltpu.SMEM)
    many = isinstance(outs, (tuple, list))
    return pl.pallas_call(
        body,
        out_shape=outs,
        in_specs=[smem] * scalars + [vmem] * (len(args) - scalars),
        out_specs=tuple(vmem for _ in outs) if many else vmem,
        cost_estimate=pl.CostEstimate(flops=flops, bytes_accessed=moved, transcendentals=0),
        compiler_params=pltpu.CompilerParams(vmem_limit_bytes=16 * MIB),
        name=body.__name__,
    )(*args)


def shape(*dims, dtype=BF):
    return jax.ShapeDtypeStruct(dims, dtype)


def lane_order(me):
    i, j = iota((512, 512), 0), iota((512, 512), 1)
    core = jnp.bitwise_xor((i // 64) % 2, me)
    hit = (
        (i // 128 == (j // F) % 4)
        & (core == j // 256)
        & ((i // F) % 2 == (j // 128) % 2)
        & (i % F == j % F)
    )
    return jnp.where(hit, 1.0, 0.0).astype(BF)


def weights_kernel(me_ref, gate_ref, up_ref, down_ref, gu_ref, dn_ref):
    order = lane_order(me_ref[0])
    gu_ref[...] = jnp.zeros_like(gu_ref)
    dn_ref[...] = jnp.zeros_like(dn_ref)
    hidden = gate_ref.shape[0]
    for ref, out, base in ((gate_ref, gu_ref, 0), (up_ref, gu_ref, 128), (down_ref, dn_ref, 0)):
        for xh in range(2):
            for zq in range(4):
                tiles = [
                    ref[:, pl.ds((zq * 4 + zi) * 256 + xh * 128, 128)] for zi in range(4)
                ]
                moved = dot(jnp.concatenate(tiles, axis=1), order).astype(BF)
                for o in range(2):
                    for h in range(2):
                        out[o, xh, pl.ds(base, hidden), pl.ds(h * 512 + zq * 128, 128)] = moved[
                            :, (o * 2 + h) * 128 : (o * 2 + h + 1) * 128
                        ]


def pack_kernel(x_ref, g_ref, out_ref):
    x = x_ref[...]
    toks, feats = x.shape
    twice = jnp.concatenate([x, x], axis=0)
    keep = iota(twice.shape, 1) // F == iota(twice.shape, 0) // toks
    twice = jnp.where(keep, twice, jnp.zeros_like(twice))
    pick = jnp.where(iota((F, feats), 1) % F == iota((F, feats), 0), 1.0, 0.0).astype(BF)
    block = jnp.concatenate([dot_last(pick, twice).astype(BF), g_ref[...]], axis=0)
    for z in range(out_ref.shape[0]):
        out_ref[z] = block


def placed(routes, rows, capacity, tokens):
    lanes = routes.shape[1]
    expert = iota((rows, lanes), 0) // capacity
    slot = iota((rows, lanes), 0) % capacity
    first, second = routes[0:1, :] == expert, routes[1:2, :] == expert
    named = first | second
    i, j = iota((lanes, lanes), 0), iota((lanes, lanes), 1)
    earlier = jnp.where((i < tokens) & (i < j % tokens), 1.0, 0.0).astype(BF)
    before = dot(jnp.where(named, 1.0, 0.0).astype(BF), earlier)
    return named & (before == slot.astype(F32)), first, second


def tables_kernel(
    routes_b_ref, gates_b_ref, routes_a_ref, gates_a_ref, picks_b_ref, mix_ref, picks_a_ref, weight_a_ref
):
    def weights(hit, first, second, gates):
        named = jnp.where(first, gates[0:1, :], 0.0) + jnp.where(second, gates[1:2, :], 0.0)
        return jnp.where(hit, named, 0.0)

    routes, gates = routes_b_ref[...], gates_b_ref[...]
    toks = routes.shape[1] // 2
    hit, first, second = placed(routes, picks_b_ref.shape[1], CAP_B, toks)
    lane = iota(hit.shape, 1) // toks
    for h in range(2):
        picks_b_ref[h] = jnp.where(hit & (lane == h), 1.0, 0.0).astype(BF)
    weight = weights(hit, first, second, gates).T[:toks]
    high = weight.astype(BF)
    rest = weight - high.astype(F32)
    middle = rest.astype(BF)
    mix_ref[0] = high
    mix_ref[1] = middle
    mix_ref[2] = (rest - middle.astype(F32)).astype(BF)

    routes, gates = routes_a_ref[...], gates_a_ref[...]
    hit, first, second = placed(routes, picks_a_ref.shape[0], CAP_A, routes.shape[1])
    picks_a_ref[...] = jnp.where(hit, 1.0, 0.0).astype(BF)
    weight = jnp.sum(weights(hit, first, second, gates), axis=1, keepdims=True)
    weight_a_ref[...] = jnp.broadcast_to(weight, weight_a_ref.shape)


def rows_new_kernel(picks_ref, got_ref, out_ref):
    experts, _, slots, width = out_ref.shape
    x = got_ref[:, 0:F, :].reshape(-1, picks_ref.shape[2])
    for h in range(2):
        block = dot_last(picks_ref[h], x).astype(BF).reshape(experts, slots, -1)
        for xh in range(2):
            out_ref[:, xh, :, h * (width // 2) : (h + 1) * (width // 2)] = block


def pick_old(picks_ref, weight_ref, ref, base, h):
    g = ref[:, base + F * h : base + F * (1 + h), :].reshape(-1, picks_ref.shape[1])
    return (dot_last(picks_ref[...], g) * weight_ref[:, 0:1]).astype(BF)


def near_rows_kernel(picks_ref, weight_ref, got_ref, out_ref):
    experts, slots, width = out_ref.shape
    for h in range(2):
        block = pick_old(picks_ref, weight_ref, got_ref, F, h).reshape(experts, slots, -1)
        out_ref[:, :, h * (width // 2) : (h + 1) * (width // 2)] = block


def far_rows_kernel(me_ref, picks_ref, weight_ref, far_ref, near_ref, out_ref):
    experts, _, slots, width = out_ref.shape
    mine = me_ref[1]
    out_ref[:, mine] = near_ref[...]
    for h in range(2):
        block = pick_old(picks_ref, weight_ref, far_ref, 0, h).reshape(experts, slots, -1)
        out_ref[:, 1 - mine, :, h * (width // 2) : (h + 1) * (width // 2)] = block


def up_kernel(own_ref, other_ref, gu_ref, dn_ref, hidden_ref, out_ref):
    total = None
    for o, ref in enumerate((own_ref, other_ref)):
        for xh in range(2):
            term = dot_last(rows_of(ref, xh), gu_ref[o, xh])
            total = term if total is None else total + term
    gate, up = total[:, :128], total[:, 128:]
    hidden = (gate / (1.0 + jnp.exp(-gate)) * up).astype(BF)
    hidden_ref[...] = hidden
    groups, _, slots, width = out_ref.shape
    for xh in range(2):
        out_ref[:, xh] = dot(hidden, dn_ref[1, xh]).astype(BF).reshape(groups, slots, width)


def down_kernel(hidden_ref, dn_ref, arrived_ref, out_ref):
    hidden = hidden_ref[...]
    groups, _, slots, width = out_ref.shape
    for xh in range(2):
        total = dot(hidden, dn_ref[0, xh]) + rows_of(arrived_ref, xh).astype(F32)
        out_ref[:, xh] = total.astype(BF).reshape(groups, slots, width)


def mix_kernel(mix_ref, got_ref, out_ref):
    width = got_ref.shape[3] // 2
    for xh in range(2):
        rows = rows_of(got_ref, xh)
        halves = []
        for h in range(2):
            got = rows[:, h * width : (h + 1) * width]
            halves.append(dot(mix_ref[0], got) + dot(mix_ref[1], got) + dot(mix_ref[2], got))
        mixed = jnp.concatenate(halves, axis=0).T.astype(BF)
        out_ref[:, xh] = mixed.reshape(out_ref.shape[0], F, -1)


def total_kernel(got_ref, out_ref):
    total = got_ref[0].astype(F32)
    for z in range(1, got_ref.shape[0]):
        total = total + got_ref[z].astype(F32)
    turned = total.T
    toks = out_ref.shape[0]
    out_ref[...] = jnp.concatenate([turned[:toks], turned[toks:]], axis=1).astype(BF)


def rows_of(ref, xh):
    return ref[:, xh].reshape(-1, ref.shape[3])


def back_kernel(me_ref, own_ref, other_ref, dn_ref, gate_ref, up_ref, down_ref, dg_ref, du_ref, held):
    total = None
    refs = (own_ref, other_ref)
    for o, ref in enumerate(refs):
        for xh in range(2):
            term = dot_last(dn_ref[o, xh], rows_of(ref, xh))
            total = term if total is None else total + term
    gate, up = gate_ref[...].astype(F32), up_ref[...].astype(F32)
    grad = total[: gate.shape[0]]
    sigma = 1.0 / (1.0 + jnp.exp(-gate))
    active = gate * sigma
    dg_ref[...] = (grad * up * sigma * (1.0 + gate * (1.0 - sigma))).astype(BF)
    du_ref[...] = (grad * active).astype(BF)
    hidden = (active * up).astype(BF)
    for o, ref in enumerate(refs):
        for xh in range(2):
            held[o, xh] = dot(hidden, rows_of(ref, xh)).astype(BF)
    order = lane_order(me_ref[0])
    for xh in range(2):
        for zq in range(4):
            tiles = [
                held[o, xh, :, pl.ds(h * 512 + zq * 128, 128)] for o in range(2) for h in range(2)
            ]
            moved = dot_last(jnp.concatenate(tiles, axis=1), order).astype(BF)
            for zi in range(4):
                down_ref[:, pl.ds((zq * 4 + zi) * 256 + xh * 128, 128)] = moved[
                    :, zi * 128 : (zi + 1) * 128
                ]


def other_core(array):
    return lax.ppermute(array, CORE, [(0, 1), (1, 0)])


def exchange(array, axes):
    peers = array.reshape(lax.axis_size(axes), -1, array.shape[-1])
    return lax.all_to_all(peers, axes, 0, 0, tiled=True).reshape(array.shape)


def per_device(
    x_new,
    routes_new,
    gates_new,
    w_gate,
    w_up,
    w_down,
    grad_out,
    routes_old,
    gates_old,
    pre_gate,
    pre_up,
):
    me = jnp.stack([lax.axis_index(CORE), lax.axis_index(XH)]).astype(jnp.int32)
    experts = lax.axis_size(EXPERT)
    rows_new, rows_old = experts * CAP_B, experts * CAP_A
    hidden_units = w_gate.shape[2]
    twice = lambda a: jnp.concatenate([a.T, a.T], axis=1)
    routes_b, gates_b = twice(routes_new), twice(gates_new)
    routes_a, gates_a = routes_old.T, gates_old.T

    packed = call(pack_kernel, shape(16, 3 * F, 128), x_new, grad_out.T)
    got = lax.all_to_all(packed, Z, 0, 0, tiled=True)
    gate_up, down = call(
        weights_kernel,
        (shape(2, 2, 256, 1024), shape(2, 2, 128, 1024)),
        me,
        w_gate[0].T,
        w_up[0].T,
        w_down[0],
        scalars=1,
        flops=14 * 10**8,
        moved=6 * 10**6,
    )

    picks_b, mix, picks_a, weight_a = call(
        tables_kernel,
        (
            shape(2, rows_new, 128),
            shape(3, x_new.shape[0], rows_new),
            shape(rows_old, 128),
            shape(rows_old, 128, dtype=F32),
        ),
        routes_b,
        gates_b,
        routes_a,
        gates_a,
    )
    got, gate_up, down, picks_b, mix, picks_a, weight_a = lax.optimization_barrier(
        (got, gate_up, down, picks_b, mix, picks_a, weight_a)
    )

    rows_b = shape(experts, 2, CAP_B, 1024)
    own = exchange(call(rows_new_kernel, rows_b, picks_b, got), PLANE)
    far = lax.ppermute(got[:, F:], XH, [(0, 1), (1, 0)])
    rows_a = shape(experts, 2, CAP_A, 1024)
    near = call(near_rows_kernel, shape(experts, CAP_A, 1024), picks_a, weight_a, got)
    begun = call(far_rows_kernel, rows_a, me, picks_a, weight_a, far, near, scalars=1)
    own, begun = lax.optimization_barrier((own, begun))
    own_a = lax.all_to_all(begun, EXPERT, 0, 0, tiled=True)

    hidden, partial = call(
        up_kernel,
        (shape(rows_new, 128), rows_b),
        own,
        other_core(own),
        gate_up,
        down,
        flops=8 * 10**8,
        moved=4 * 10**6,
    )
    summed = call(down_kernel, rows_b, hidden, down, other_core(partial), flops=2 * 10**8)
    own_a, summed = lax.optimization_barrier((own_a, summed))
    returned = exchange(summed, EXPERT)

    other_a = other_core(own_a)
    vmem = pl.BlockSpec(memory_space=pltpu.VMEM)
    weight_grad, gate_grad, up_grad = pl.pallas_call(
        back_kernel,
        out_shape=(
            shape(hidden_units, 4096),
            shape(hidden_units, rows_old),
            shape(hidden_units, rows_old),
        ),
        in_specs=[pl.BlockSpec(memory_space=pltpu.SMEM)] + [vmem] * 5,
        out_specs=(vmem,) * 3,
        scratch_shapes=[pltpu.VMEM((2, 2, hidden_units, 1024), BF)],
        cost_estimate=pl.CostEstimate(
            flops=15 * 10**8, bytes_accessed=8 * 10**6, transcendentals=0
        ),
        compiler_params=pltpu.CompilerParams(vmem_limit_bytes=16 * MIB),
        name="back_kernel",
    )(me, own_a, other_a, down, pre_gate[0].T, pre_up[0].T)
    returned, weight_grad, gate_grad, up_grad = lax.optimization_barrier(
        (returned, weight_grad, gate_grad, up_grad)
    )

    mixed = call(mix_kernel, shape(16, 2, F, 128), mix, returned, flops=4 * 10**8)
    mixed = exchange(mixed.reshape(32, F, 128), Z_XH)
    mixed = call(total_kernel, shape(*x_new.shape), mixed)
    return (mixed, weight_grad[None], gate_grad.T[None], up_grad.T[None])


def solution(mesh):
    torus = Mesh(
        mesh.devices.reshape(4, 2, 16, 2, 2), ("expert_0", "expert_1", "dp_0", "dp_1", "dp_2")
    )
    placed_as = (
        P(EXPERT, DP),
        P(EXPERT, None),
        P(EXPERT, None),
        P(EXPERT, None, DP),
        P(EXPERT, None, DP),
        P(EXPERT, DP, None),
        P(EXPERT, DP),
        P(EXPERT, None),
        P(EXPERT, None),
        P(EXPERT, None, DP),
        P(EXPERT, None, DP),
    )
    return jax.shard_map(
        per_device,
        mesh=torus,
        in_specs=placed_as,
        out_specs=(P(EXPERT, DP), P(EXPERT, DP, None), P(EXPERT, None, DP), P(EXPERT, None, DP)),
        check_vma=False,
    )
```

```python
import functools

import jax
import jax.numpy as jnp
from jax import lax
from jax.experimental import pallas as pl
from jax.experimental.pallas import tpu as pltpu
from jax.sharding import Mesh
from jax.sharding import PartitionSpec as P

CAP_B = 32
CAP_A = 64
EXPERT = ("expert_0", "expert_1")
DP = ("dp_0", "dp_1", "dp_2")
Z = "dp_0"
CORE = "dp_2"
PLANE = ("expert_0", "expert_1", "dp_1")
F = 32
BF = jnp.bfloat16
F32 = jnp.float32
LAST = (((1,), (1,)), ((), ()))
MIB = 1 << 20


def iota(shape, dim):
    return lax.broadcasted_iota(jnp.int32, shape, dim)


def dot(a, b):
    return jnp.dot(a, b, preferred_element_type=F32)


def dot_last(a, b):
    return lax.dot_general(a, b, LAST, preferred_element_type=F32)


def call(body, outs, *args, flops=10**7, moved=10**6, scalars=0):
    vmem = pl.BlockSpec(memory_space=pltpu.VMEM)
    smem = pl.BlockSpec(memory_space=pltpu.SMEM)
    many = isinstance(outs, (tuple, list))
    return pl.pallas_call(
        body,
        out_shape=outs,
        in_specs=[smem] * scalars + [vmem] * (len(args) - scalars),
        out_specs=tuple(vmem for _ in outs) if many else vmem,
        cost_estimate=pl.CostEstimate(flops=flops, bytes_accessed=moved, transcendentals=0),
        compiler_params=pltpu.CompilerParams(vmem_limit_bytes=16 * MIB),
        name=body.__name__,
    )(*args)


def shape(*dims, dtype=BF):
    return jax.ShapeDtypeStruct(dims, dtype)


def lane_order(me):
    i, j = iota((512, 512), 0), iota((512, 512), 1)
    core = jnp.bitwise_xor((i // 64) % 2, me)
    hit = (
        (i // 128 == (j // F) % 4)
        & (core == j // 256)
        & ((i // F) % 2 == (j // 128) % 2)
        & (i % F == j % F)
    )
    return jnp.where(hit, 1.0, 0.0).astype(BF)


def weights_kernel(me_ref, gate_ref, up_ref, down_ref, gu_ref, dn_ref):
    order = lane_order(me_ref[0])
    gu_ref[...] = jnp.zeros_like(gu_ref)
    dn_ref[...] = jnp.zeros_like(dn_ref)
    hidden = gate_ref.shape[0]
    for ref, out, base in ((gate_ref, gu_ref, 0), (up_ref, gu_ref, 128), (down_ref, dn_ref, 0)):
        for xh in range(2):
            for zq in range(4):
                tiles = [
                    ref[:, pl.ds((zq * 4 + zi) * 256 + xh * 128, 128)] for zi in range(4)
                ]
                moved = dot(jnp.concatenate(tiles, axis=1), order).astype(BF)
                for o in range(2):
                    for h in range(2):
                        out[o, xh, pl.ds(base, hidden), pl.ds(h * 512 + zq * 128, 128)] = moved[
                            :, (o * 2 + h) * 128 : (o * 2 + h + 1) * 128
                        ]


def pack_kernel(x_hbm, g_hbm, out_ref, x_ref, g_ref, sems):
    copies = [
        pltpu.make_async_copy(x_hbm, x_ref, sems.at[0]),
        pltpu.make_async_copy(g_hbm, g_ref, sems.at[1]),
    ]
    for copy in copies:
        copy.start()
    for copy in copies:
        copy.wait()
    x = x_ref[...]
    toks, feats = x.shape
    twice = jnp.concatenate([x, x], axis=0)
    keep = iota(twice.shape, 1) // F == iota(twice.shape, 0) // toks
    twice = jnp.where(keep, twice, jnp.zeros_like(twice))
    pick = jnp.where(iota((F, feats), 1) % F == iota((F, feats), 0), 1.0, 0.0).astype(BF)
    block = jnp.concatenate([dot_last(pick, twice).astype(BF), g_ref[...]], axis=0)
    for z in range(out_ref.shape[0]):
        out_ref[z] = block


def placed(routes, rows, capacity, tokens):
    lanes = routes.shape[1]
    expert = iota((rows, lanes), 0) // capacity
    slot = iota((rows, lanes), 0) % capacity
    first, second = routes[0:1, :] == expert, routes[1:2, :] == expert
    named = first | second
    i, j = iota((lanes, lanes), 0), iota((lanes, lanes), 1)
    earlier = jnp.where((i < tokens) & (i < j % tokens), 1.0, 0.0).astype(BF)
    before = dot(jnp.where(named, 1.0, 0.0).astype(BF), earlier)
    return named & (before == slot.astype(F32)), first, second


def tables_kernel(
    routes_b_ref, gates_b_ref, routes_a_ref, gates_a_ref, picks_b_ref, mix_ref, picks_a_ref, weight_a_ref
):
    def weights(hit, first, second, gates):
        named = jnp.where(first, gates[0:1, :], 0.0) + jnp.where(second, gates[1:2, :], 0.0)
        return jnp.where(hit, named, 0.0)

    routes, gates = routes_b_ref[...], gates_b_ref[...]
    toks = routes.shape[1] // 2
    hit, first, second = placed(routes, picks_b_ref.shape[1], CAP_B, toks)
    lane = iota(hit.shape, 1) // toks
    for h in range(2):
        picks_b_ref[h] = jnp.where(hit & (lane == h), 1.0, 0.0).astype(BF)
    weight = weights(hit, first, second, gates).T[:toks]
    high = weight.astype(BF)
    rest = weight - high.astype(F32)
    middle = rest.astype(BF)
    mix_ref[0] = high
    mix_ref[1] = middle
    mix_ref[2] = (rest - middle.astype(F32)).astype(BF)

    routes, gates = routes_a_ref[...], gates_a_ref[...]
    hit, first, second = placed(routes, picks_a_ref.shape[0], CAP_A, routes.shape[1])
    picks_a_ref[...] = jnp.where(hit, 1.0, 0.0).astype(BF)
    weight = jnp.sum(weights(hit, first, second, gates), axis=1, keepdims=True)
    weight_a_ref[...] = jnp.broadcast_to(weight, weight_a_ref.shape)


def rows_new_kernel(picks_ref, got_ref, out_ref):
    experts, _, slots, width = out_ref.shape
    x = got_ref[:, 0:F, :].reshape(-1, picks_ref.shape[2])
    for h in range(2):
        block = dot_last(picks_ref[h], x).astype(BF).reshape(experts, slots, -1)
        for xh in range(2):
            out_ref[:, xh, :, h * (width // 2) : (h + 1) * (width // 2)] = block


def rows_old_kernel(picks_ref, weight_ref, got_ref, out_ref):
    experts, _, slots, width = out_ref.shape
    for h in range(2):
        g = got_ref[:, F * (1 + h) : F * (2 + h), :].reshape(-1, picks_ref.shape[1])
        block = (dot_last(picks_ref[...], g) * weight_ref[:, 0:1]).astype(BF)
        block = block.reshape(experts, slots, -1)
        for xh in range(2):
            out_ref[:, xh, :, h * (width // 2) : (h + 1) * (width // 2)] = block


def up_kernel(own_ref, other_ref, gu_ref, dn_ref, hidden_ref, out_ref):
    total = None
    for o, ref in enumerate((own_ref, other_ref)):
        for xh in range(2):
            term = dot_last(rows_of(ref, xh), gu_ref[o, xh])
            total = term if total is None else total + term
    gate, up = total[:, :128], total[:, 128:]
    hidden = (gate / (1.0 + jnp.exp(-gate)) * up).astype(BF)
    hidden_ref[...] = hidden
    groups, _, slots, width = out_ref.shape
    for xh in range(2):
        out_ref[:, xh] = dot(hidden, dn_ref[1, xh]).astype(BF).reshape(groups, slots, width)


def down_kernel(hidden_ref, dn_ref, arrived_ref, out_ref):
    hidden = hidden_ref[...]
    groups, _, slots, width = out_ref.shape
    for xh in range(2):
        total = dot(hidden, dn_ref[0, xh]) + rows_of(arrived_ref, xh).astype(F32)
        out_ref[:, xh] = total.astype(BF).reshape(groups, slots, width)


def mix_kernel(mix_ref, got_ref, out_ref):
    width = got_ref.shape[3] // 2
    rows = [rows_of(got_ref, xh) for xh in range(2)]
    halves = []
    for h in range(2):
        total = None
        for xh in range(2):
            for part in range(3):
                term = dot(mix_ref[part], rows[xh][:, h * width : (h + 1) * width])
                total = term if total is None else total + term
        halves.append(total)
    mixed = jnp.concatenate(halves, axis=0).T.astype(BF)
    out_ref[...] = mixed.reshape(out_ref.shape)


def total_kernel(got_ref, out_ref):
    total = got_ref[0].astype(F32)
    for z in range(1, got_ref.shape[0]):
        total = total + got_ref[z].astype(F32)
    turned = total.T
    toks = out_ref.shape[0]
    out_ref[...] = jnp.concatenate([turned[:toks], turned[toks:]], axis=1).astype(BF)


def rows_of(ref, xh):
    return ref[:, xh].reshape(-1, ref.shape[3])


def back_kernel(
    me_ref, own_ref, other_ref, dn_ref, gate_ref, up_ref, down_ref, dg_ref, du_ref, held
):
    refs = (own_ref, other_ref)
    total = None
    for o, ref in enumerate(refs):
        for xh in range(2):
            term = dot_last(dn_ref[o, xh], rows_of(ref, xh))
            total = term if total is None else total + term
    gate, up = gate_ref[...].astype(F32), up_ref[...].astype(F32)
    grad = total[: gate.shape[0]]
    sigma = 1.0 / (1.0 + jnp.exp(-gate))
    active = gate * sigma
    dg_ref[...] = (grad * up * sigma * (1.0 + gate * (1.0 - sigma))).astype(BF)
    du_ref[...] = (grad * active).astype(BF)
    hidden = (active * up).astype(BF)
    for o, ref in enumerate(refs):
        for xh in range(2):
            held[o, xh] = dot(hidden, rows_of(ref, xh)).astype(BF)
    order = lane_order(me_ref[0])
    for xh in range(2):
        for zq in range(4):
            tiles = [
                held[o, xh, :, pl.ds(h * 512 + zq * 128, 128)] for o in range(2) for h in range(2)
            ]
            moved = dot_last(jnp.concatenate(tiles, axis=1), order).astype(BF)
            for zi in range(4):
                down_ref[:, pl.ds((zq * 4 + zi) * 256 + xh * 128, 128)] = moved[
                    :, zi * 128 : (zi + 1) * 128
                ]


def other_core(array):
    return lax.ppermute(array, CORE, [(0, 1), (1, 0)])


def exchange(array, axes):
    peers = array.reshape(lax.axis_size(axes), -1, array.shape[-1])
    return lax.all_to_all(peers, axes, 0, 0, tiled=True).reshape(array.shape)


def per_device(
    x_new,
    routes_new,
    gates_new,
    w_gate,
    w_up,
    w_down,
    grad_out,
    routes_old,
    gates_old,
    pre_gate,
    pre_up,
):
    me = lax.axis_index(CORE).astype(jnp.int32).reshape(1)
    experts = lax.axis_size(EXPERT)
    rows_new, rows_old = experts * CAP_B, experts * CAP_A
    hidden_units = w_gate.shape[2]
    twice = lambda a: jnp.concatenate([a.T, a.T], axis=1)
    routes_b, gates_b = twice(routes_new), twice(gates_new)
    routes_a, gates_a = routes_old.T, gates_old.T

    packed = pl.pallas_call(
        pack_kernel,
        out_shape=shape(16, 3 * F, 128),
        in_specs=[pl.BlockSpec(memory_space=pltpu.HBM)] * 2,
        out_specs=pl.BlockSpec(memory_space=pltpu.VMEM),
        scratch_shapes=[
            pltpu.VMEM(x_new.shape, BF),
            pltpu.VMEM(grad_out.shape[::-1], BF),
            pltpu.SemaphoreType.DMA((2,)),
        ],
        compiler_params=pltpu.CompilerParams(vmem_limit_bytes=16 * MIB),
        name="pack_kernel",
    )(x_new, grad_out.T)
    got = lax.all_to_all(packed, Z, 0, 0, tiled=True)
    gate_up, down = call(
        weights_kernel,
        (shape(2, 2, 256, 1024), shape(2, 2, 128, 1024)),
        me,
        w_gate[0].T,
        w_up[0].T,
        w_down[0],
        scalars=1,
        flops=14 * 10**8,
        moved=6 * 10**6,
    )

    picks_b, mix, picks_a, weight_a = call(
        tables_kernel,
        (
            shape(2, rows_new, 128),
            shape(3, x_new.shape[0], rows_new),
            shape(rows_old, 128),
            shape(rows_old, 128, dtype=F32),
        ),
        routes_b,
        gates_b,
        routes_a,
        gates_a,
    )
    got, gate_up, down, picks_b, mix, picks_a, weight_a = lax.optimization_barrier(
        (got, gate_up, down, picks_b, mix, picks_a, weight_a)
    )

    rows_b = shape(experts, 2, CAP_B, 1024)
    own = exchange(call(rows_new_kernel, rows_b, picks_b, got), PLANE)
    rows_a = shape(experts, 2, CAP_A, 1024)
    sent_a = call(rows_old_kernel, rows_a, picks_a, weight_a, got)
    own_a = exchange(sent_a, PLANE)

    hidden, partial = call(
        up_kernel,
        (shape(rows_new, 128), rows_b),
        own,
        other_core(own),
        gate_up,
        down,
        flops=8 * 10**8,
        moved=4 * 10**6,
    )
    summed = call(down_kernel, rows_b, hidden, down, other_core(partial), flops=2 * 10**8)
    returned = exchange(summed, PLANE)

    other_a = other_core(own_a)
    vmem = pl.BlockSpec(memory_space=pltpu.VMEM)
    weight_grad, gate_grad, up_grad = pl.pallas_call(
        back_kernel,
        out_shape=(
            shape(hidden_units, 4096),
            shape(hidden_units, rows_old),
            shape(hidden_units, rows_old),
        ),
        in_specs=[pl.BlockSpec(memory_space=pltpu.SMEM)] + [vmem] * 5,
        out_specs=(vmem,) * 3,
        scratch_shapes=[pltpu.VMEM((2, 2, hidden_units, 1024), BF)],
        cost_estimate=pl.CostEstimate(
            flops=15 * 10**8, bytes_accessed=8 * 10**6, transcendentals=0
        ),
        compiler_params=pltpu.CompilerParams(vmem_limit_bytes=16 * MIB),
        name="back_kernel",
    )(me, own_a, other_a, down, pre_gate[0].T, pre_up[0].T)
    mixed = call(mix_kernel, shape(16, F, 128), mix, returned, flops=4 * 10**8)
    mixed = exchange(mixed, Z)
    mixed, weight_grad, gate_grad, up_grad = lax.optimization_barrier(
        (mixed, weight_grad, gate_grad, up_grad)
    )
    mixed = call(total_kernel, shape(*x_new.shape), mixed)
    return (mixed, weight_grad[None], gate_grad.T[None], up_grad.T[None])


def solution(mesh):
    torus = Mesh(
        mesh.devices.reshape(4, 2, 16, 2, 2), ("expert_0", "expert_1", "dp_0", "dp_1", "dp_2")
    )
    placed_as = (
        P(EXPERT, DP),
        P(EXPERT, None),
        P(EXPERT, None),
        P(EXPERT, None, DP),
        P(EXPERT, None, DP),
        P(EXPERT, DP, None),
        P(EXPERT, DP),
        P(EXPERT, None),
        P(EXPERT, None),
        P(EXPERT, None, DP),
        P(EXPERT, None, DP),
    )
    return jax.shard_map(
        per_device,
        mesh=torus,
        in_specs=placed_as,
        out_specs=(P(EXPERT, DP), P(EXPERT, DP, None), P(EXPERT, None, DP), P(EXPERT, None, DP)),
        check_vma=False,
    )
```

```python
import functools

import jax
import jax.numpy as jnp
from jax import lax
from jax.experimental import pallas as pl
from jax.experimental.pallas import tpu as pltpu
from jax.sharding import Mesh
from jax.sharding import PartitionSpec as P

CAP_B = 32
CAP_A = 64
EXPERT = ("expert_0", "expert_1")
DP = ("dp_0", "dp_1", "dp_2")
Z = "dp_0"
CORE = "dp_2"
PLANE = ("expert_0", "expert_1", "dp_1")
F = 32
BF = jnp.bfloat16
F32 = jnp.float32
LAST = (((1,), (1,)), ((), ()))
MIB = 1 << 20


def iota(shape, dim):
    return lax.broadcasted_iota(jnp.int32, shape, dim)


def dot(a, b):
    return jnp.dot(a, b, preferred_element_type=F32)


def dot_last(a, b):
    return lax.dot_general(a, b, LAST, preferred_element_type=F32)


def call(body, outs, *args, flops=10**7, moved=10**6, scalars=0):
    vmem = pl.BlockSpec(memory_space=pltpu.VMEM)
    smem = pl.BlockSpec(memory_space=pltpu.SMEM)
    many = isinstance(outs, (tuple, list))
    return pl.pallas_call(
        body,
        out_shape=outs,
        in_specs=[smem] * scalars + [vmem] * (len(args) - scalars),
        out_specs=tuple(vmem for _ in outs) if many else vmem,
        cost_estimate=pl.CostEstimate(flops=flops, bytes_accessed=moved, transcendentals=0),
        compiler_params=pltpu.CompilerParams(vmem_limit_bytes=16 * MIB),
        name=body.__name__,
    )(*args)


def shape(*dims, dtype=BF):
    return jax.ShapeDtypeStruct(dims, dtype)


def lane_order(me):
    i, j = iota((512, 512), 0), iota((512, 512), 1)
    core = jnp.bitwise_xor((i // 64) % 2, me)
    hit = (
        (i // 128 == (j // F) % 4)
        & (core == j // 256)
        & ((i // F) % 2 == (j // 128) % 2)
        & (i % F == j % F)
    )
    return jnp.where(hit, 1.0, 0.0).astype(BF)


def weights_kernel(me_ref, gate_ref, up_ref, down_ref, gu_ref, dn_ref):
    order = lane_order(me_ref[0])
    gu_ref[...] = jnp.zeros_like(gu_ref)
    dn_ref[...] = jnp.zeros_like(dn_ref)
    hidden = gate_ref.shape[0]
    for ref, out, base in ((gate_ref, gu_ref, 0), (up_ref, gu_ref, 128), (down_ref, dn_ref, 0)):
        for xh in range(2):
            for zq in range(4):
                tiles = [
                    ref[:, pl.ds((zq * 4 + zi) * 256 + xh * 128, 128)] for zi in range(4)
                ]
                moved = dot(jnp.concatenate(tiles, axis=1), order).astype(BF)
                for o in range(2):
                    for h in range(2):
                        out[o, xh, pl.ds(base, hidden), pl.ds(h * 512 + zq * 128, 128)] = moved[
                            :, (o * 2 + h) * 128 : (o * 2 + h + 1) * 128
                        ]


def pack_kernel(x_hbm, g_hbm, out_ref, x_ref, g_ref, sems):
    copies = [
        pltpu.make_async_copy(x_hbm, x_ref, sems.at[0]),
        pltpu.make_async_copy(g_hbm, g_ref, sems.at[1]),
    ]
    for copy in copies:
        copy.start()
    for copy in copies:
        copy.wait()
    x = x_ref[...]
    toks, feats = x.shape
    twice = jnp.concatenate([x, x], axis=0)
    keep = iota(twice.shape, 1) // F == iota(twice.shape, 0) // toks
    twice = jnp.where(keep, twice, jnp.zeros_like(twice))
    pick = jnp.where(iota((F, feats), 1) % F == iota((F, feats), 0), 1.0, 0.0).astype(BF)
    x = dot_last(pick, twice).astype(BF)
    blocks = [jnp.concatenate([x, g_ref[F * h : F * (h + 1)]], axis=0) for h in range(2)]
    for z in range(out_ref.shape[0]):
        out_ref[z] = blocks[z % 2]


def placed(routes, rows, capacity, tokens):
    lanes = routes.shape[1]
    expert = iota((rows, lanes), 0) // capacity
    slot = iota((rows, lanes), 0) % capacity
    first, second = routes[0:1, :] == expert, routes[1:2, :] == expert
    named = first | second
    i, j = iota((lanes, lanes), 0), iota((lanes, lanes), 1)
    earlier = jnp.where((i < tokens) & (i < j % tokens), 1.0, 0.0).astype(BF)
    before = dot(jnp.where(named, 1.0, 0.0).astype(BF), earlier)
    return named & (before == slot.astype(F32)), first, second


def tables_kernel(
    routes_b_ref, gates_b_ref, routes_a_ref, gates_a_ref, picks_b_ref, mix_ref, picks_a_ref, weight_a_ref
):
    def weights(hit, first, second, gates):
        named = jnp.where(first, gates[0:1, :], 0.0) + jnp.where(second, gates[1:2, :], 0.0)
        return jnp.where(hit, named, 0.0)

    routes, gates = routes_b_ref[...], gates_b_ref[...]
    toks = routes.shape[1] // 2
    hit, first, second = placed(routes, picks_b_ref.shape[1], CAP_B, toks)
    lane = iota(hit.shape, 1) // toks
    for h in range(2):
        picks_b_ref[h] = jnp.where(hit & (lane == h), 1.0, 0.0).astype(BF)
    weight = weights(hit, first, second, gates).T[:toks]
    high = weight.astype(BF)
    rest = weight - high.astype(F32)
    middle = rest.astype(BF)
    mix_ref[0] = high
    mix_ref[1] = middle
    mix_ref[2] = (rest - middle.astype(F32)).astype(BF)

    routes, gates = routes_a_ref[...], gates_a_ref[...]
    hit, first, second = placed(routes, picks_a_ref.shape[0], CAP_A, routes.shape[1])
    picks_a_ref[...] = jnp.where(hit, 1.0, 0.0).astype(BF)
    weight = jnp.sum(weights(hit, first, second, gates), axis=1, keepdims=True)
    weight_a_ref[...] = jnp.broadcast_to(weight, weight_a_ref.shape)


def rows_new_kernel(picks_ref, got_ref, out_ref):
    experts, _, slots, width = out_ref.shape
    x = got_ref[:, 0:F, :].reshape(-1, picks_ref.shape[2])
    for h in range(2):
        block = dot_last(picks_ref[h], x).astype(BF).reshape(experts, slots, -1)
        for xh in range(2):
            out_ref[:, xh, :, h * (width // 2) : (h + 1) * (width // 2)] = block


def rows_old_kernel(me_ref, picks_ref, weight_ref, got_ref, other_ref, out_ref):
    experts, _, slots, width = out_ref.shape
    even = me_ref[1] == 0
    mine = got_ref[:, F : 2 * F, :].reshape(-1, picks_ref.shape[1])
    other = other_ref[...].reshape(mine.shape)
    for h in range(2):
        g = jnp.where(even, mine, other) if h == 0 else jnp.where(even, other, mine)
        block = (dot_last(picks_ref[...], g) * weight_ref[:, 0:1]).astype(BF)
        block = block.reshape(experts, slots, -1)
        for xh in range(2):
            out_ref[:, xh, :, h * (width // 2) : (h + 1) * (width // 2)] = block


def up_kernel(own_ref, other_ref, gu_ref, dn_ref, hidden_ref, out_ref):
    total = None
    for o, ref in enumerate((own_ref, other_ref)):
        for xh in range(2):
            term = dot_last(rows_of(ref, xh), gu_ref[o, xh])
            total = term if total is None else total + term
    gate, up = total[:, :128], total[:, 128:]
    hidden = (gate / (1.0 + jnp.exp(-gate)) * up).astype(BF)
    hidden_ref[...] = hidden
    groups, _, slots, width = out_ref.shape
    for xh in range(2):
        out_ref[:, xh] = dot(hidden, dn_ref[1, xh]).astype(BF).reshape(groups, slots, width)


def down_kernel(hidden_ref, dn_ref, arrived_ref, out_ref):
    hidden = hidden_ref[...]
    groups, _, slots, width = out_ref.shape
    for xh in range(2):
        total = dot(hidden, dn_ref[0, xh]) + rows_of(arrived_ref, xh).astype(F32)
        out_ref[:, xh] = total.astype(BF).reshape(groups, slots, width)


def mix_kernel(mix_ref, got_ref, out_ref):
    width = got_ref.shape[3] // 2
    rows = [rows_of(got_ref, xh) for xh in range(2)]
    halves = []
    for h in range(2):
        total = None
        for xh in range(2):
            for part in range(3):
                term = dot(mix_ref[part], rows[xh][:, h * width : (h + 1) * width])
                total = term if total is None else total + term
        halves.append(total)
    mixed = jnp.concatenate(halves, axis=0).T.astype(BF)
    out_ref[...] = mixed.reshape(out_ref.shape)


def total_kernel(got_ref, out_ref):
    total = got_ref[0].astype(F32)
    for z in range(1, got_ref.shape[0]):
        total = total + got_ref[z].astype(F32)
    turned = total.T
    toks = out_ref.shape[0]
    out_ref[...] = jnp.concatenate([turned[:toks], turned[toks:]], axis=1).astype(BF)


def rows_of(ref, xh):
    return ref[:, xh].reshape(-1, ref.shape[3])


def back_kernel(
    me_ref, own_ref, other_ref, dn_ref, gate_ref, up_ref, down_ref, dg_ref, du_ref, held
):
    refs = (own_ref, other_ref)
    total = None
    for o, ref in enumerate(refs):
        for xh in range(2):
            term = dot_last(dn_ref[o, xh], rows_of(ref, xh))
            total = term if total is None else total + term
    gate, up = gate_ref[...].astype(F32), up_ref[...].astype(F32)
    grad = total[: gate.shape[0]]
    sigma = 1.0 / (1.0 + jnp.exp(-gate))
    active = gate * sigma
    dg_ref[...] = (grad * up * sigma * (1.0 + gate * (1.0 - sigma))).astype(BF)
    du_ref[...] = (grad * active).astype(BF)
    hidden = (active * up).astype(BF)
    for o, ref in enumerate(refs):
        for xh in range(2):
            held[o, xh] = dot(hidden, rows_of(ref, xh)).astype(BF)
    order = lane_order(me_ref[0])
    for xh in range(2):
        for zq in range(4):
            tiles = [
                held[o, xh, :, pl.ds(h * 512 + zq * 128, 128)] for o in range(2) for h in range(2)
            ]
            moved = dot_last(jnp.concatenate(tiles, axis=1), order).astype(BF)
            for zi in range(4):
                down_ref[:, pl.ds((zq * 4 + zi) * 256 + xh * 128, 128)] = moved[
                    :, zi * 128 : (zi + 1) * 128
                ]


def other_core(array):
    return lax.ppermute(array, CORE, [(0, 1), (1, 0)])


def exchange(array, axes):
    peers = array.reshape(lax.axis_size(axes), -1, array.shape[-1])
    return lax.all_to_all(peers, axes, 0, 0, tiled=True).reshape(array.shape)


def per_device(
    x_new,
    routes_new,
    gates_new,
    w_gate,
    w_up,
    w_down,
    grad_out,
    routes_old,
    gates_old,
    pre_gate,
    pre_up,
):
    me = jnp.stack([lax.axis_index(CORE), lax.axis_index(Z) % 2]).astype(jnp.int32)
    experts = lax.axis_size(EXPERT)
    rows_new, rows_old = experts * CAP_B, experts * CAP_A
    hidden_units = w_gate.shape[2]
    twice = lambda a: jnp.concatenate([a.T, a.T], axis=1)
    routes_b, gates_b = twice(routes_new), twice(gates_new)
    routes_a, gates_a = routes_old.T, gates_old.T

    packed = pl.pallas_call(
        pack_kernel,
        out_shape=shape(16, 2 * F, 128),
        in_specs=[pl.BlockSpec(memory_space=pltpu.HBM)] * 2,
        out_specs=pl.BlockSpec(memory_space=pltpu.VMEM),
        scratch_shapes=[
            pltpu.VMEM(x_new.shape, BF),
            pltpu.VMEM(grad_out.shape[::-1], BF),
            pltpu.SemaphoreType.DMA((2,)),
        ],
        compiler_params=pltpu.CompilerParams(vmem_limit_bytes=16 * MIB),
        name="pack_kernel",
    )(x_new, grad_out.T)
    got = lax.all_to_all(packed, Z, 0, 0, tiled=True)
    gate_up, down = call(
        weights_kernel,
        (shape(2, 2, 256, 1024), shape(2, 2, 128, 1024)),
        me,
        w_gate[0].T,
        w_up[0].T,
        w_down[0],
        scalars=1,
        flops=14 * 10**8,
        moved=6 * 10**6,
    )

    picks_b, mix, picks_a, weight_a = call(
        tables_kernel,
        (
            shape(2, rows_new, 128),
            shape(3, x_new.shape[0], rows_new),
            shape(rows_old, 128),
            shape(rows_old, 128, dtype=F32),
        ),
        routes_b,
        gates_b,
        routes_a,
        gates_a,
    )
    got, gate_up, down, picks_b, mix, picks_a, weight_a = lax.optimization_barrier(
        (got, gate_up, down, picks_b, mix, picks_a, weight_a)
    )

    rows_b = shape(experts, 2, CAP_B, 1024)
    own = exchange(call(rows_new_kernel, rows_b, picks_b, got), PLANE)
    rows_a = shape(experts, 2, CAP_A, 1024)
    half = lax.ppermute(got[:, F:], Z, [(z, z ^ 1) for z in range(lax.axis_size(Z))])
    sent_a = call(rows_old_kernel, rows_a, me, picks_a, weight_a, got, half, scalars=1)
    own_a = exchange(sent_a, PLANE)

    hidden, partial = call(
        up_kernel,
        (shape(rows_new, 128), rows_b),
        own,
        other_core(own),
        gate_up,
        down,
        flops=8 * 10**8,
        moved=4 * 10**6,
    )
    summed = call(down_kernel, rows_b, hidden, down, other_core(partial), flops=2 * 10**8)
    returned = exchange(summed, PLANE)

    other_a = other_core(own_a)
    vmem = pl.BlockSpec(memory_space=pltpu.VMEM)
    weight_grad, gate_grad, up_grad = pl.pallas_call(
        back_kernel,
        out_shape=(
            shape(hidden_units, 4096),
            shape(hidden_units, rows_old),
            shape(hidden_units, rows_old),
        ),
        in_specs=[pl.BlockSpec(memory_space=pltpu.SMEM)] + [vmem] * 5,
        out_specs=(vmem,) * 3,
        scratch_shapes=[pltpu.VMEM((2, 2, hidden_units, 1024), BF)],
        cost_estimate=pl.CostEstimate(
            flops=15 * 10**8, bytes_accessed=8 * 10**6, transcendentals=0
        ),
        compiler_params=pltpu.CompilerParams(vmem_limit_bytes=16 * MIB),
        name="back_kernel",
    )(me, own_a, other_a, down, pre_gate[0].T, pre_up[0].T)
    mixed = call(mix_kernel, shape(16, F, 128), mix, returned, flops=4 * 10**8)
    mixed = exchange(mixed, Z)
    mixed, weight_grad, gate_grad, up_grad = lax.optimization_barrier(
        (mixed, weight_grad, gate_grad, up_grad)
    )
    mixed = call(total_kernel, shape(*x_new.shape), mixed)
    return (mixed, weight_grad[None], gate_grad.T[None], up_grad.T[None])


def solution(mesh):
    torus = Mesh(
        mesh.devices.reshape(4, 2, 16, 2, 2), ("expert_0", "expert_1", "dp_0", "dp_1", "dp_2")
    )
    placed_as = (
        P(EXPERT, DP),
        P(EXPERT, None),
        P(EXPERT, None),
        P(EXPERT, None, DP),
        P(EXPERT, None, DP),
        P(EXPERT, DP, None),
        P(EXPERT, DP),
        P(EXPERT, None),
        P(EXPERT, None),
        P(EXPERT, None, DP),
        P(EXPERT, None, DP),
    )
    return jax.shard_map(
        per_device,
        mesh=torus,
        in_specs=placed_as,
        out_specs=(P(EXPERT, DP), P(EXPERT, DP, None), P(EXPERT, None, DP), P(EXPERT, None, DP)),
        check_vma=False,
    )
```

```python
import functools

import jax
import jax.numpy as jnp
from jax import lax
from jax.experimental import pallas as pl
from jax.experimental.pallas import tpu as pltpu
from jax.sharding import Mesh
from jax.sharding import PartitionSpec as P

CAP_B = 32
CAP_A = 64
EXPERT = ("expert_0", "expert_1")
DP = ("dp_0", "dp_1", "dp_2")
Z = "dp_0"
CORE = "dp_2"
PLANE = ("expert_0", "expert_1", "dp_1")
F = 32
BF = jnp.bfloat16
F32 = jnp.float32
LAST = (((1,), (1,)), ((), ()))
MIB = 1 << 20


def iota(shape, dim):
    return lax.broadcasted_iota(jnp.int32, shape, dim)


def dot(a, b):
    return jnp.dot(a, b, preferred_element_type=F32)


def dot_last(a, b):
    return lax.dot_general(a, b, LAST, preferred_element_type=F32)


def call(body, outs, *args, flops=10**7, moved=10**6, scalars=0):
    vmem = pl.BlockSpec(memory_space=pltpu.VMEM)
    smem = pl.BlockSpec(memory_space=pltpu.SMEM)
    many = isinstance(outs, (tuple, list))
    return pl.pallas_call(
        body,
        out_shape=outs,
        in_specs=[smem] * scalars + [vmem] * (len(args) - scalars),
        out_specs=tuple(vmem for _ in outs) if many else vmem,
        cost_estimate=pl.CostEstimate(flops=flops, bytes_accessed=moved, transcendentals=0),
        compiler_params=pltpu.CompilerParams(vmem_limit_bytes=16 * MIB),
        name=body.__name__,
    )(*args)


def shape(*dims, dtype=BF):
    return jax.ShapeDtypeStruct(dims, dtype)


def lane_order(me):
    i, j = iota((512, 512), 0), iota((512, 512), 1)
    core = jnp.bitwise_xor((i // 64) % 2, me)
    hit = (
        (i // 128 == (j // F) % 4)
        & (core == j // 256)
        & ((i // F) % 2 == (j // 128) % 2)
        & (i % F == j % F)
    )
    return jnp.where(hit, 1.0, 0.0).astype(BF)


def weights_kernel(me_ref, gate_ref, up_ref, down_ref, gu_ref, dn_ref):
    order = lane_order(me_ref[0])
    gu_ref[...] = jnp.zeros_like(gu_ref)
    dn_ref[...] = jnp.zeros_like(dn_ref)
    hidden = gate_ref.shape[0]
    for ref, out, base in ((gate_ref, gu_ref, 0), (up_ref, gu_ref, 128), (down_ref, dn_ref, 0)):
        for xh in range(2):
            for zq in range(4):
                tiles = [
                    ref[:, pl.ds((zq * 4 + zi) * 256 + xh * 128, 128)] for zi in range(4)
                ]
                moved = dot(jnp.concatenate(tiles, axis=1), order).astype(BF)
                for o in range(2):
                    for h in range(2):
                        out[o, xh, pl.ds(base, hidden), pl.ds(h * 512 + zq * 128, 128)] = moved[
                            :, (o * 2 + h) * 128 : (o * 2 + h + 1) * 128
                        ]


def pack_kernel(x_hbm, g_hbm, out_ref, x_ref, g_ref, sems):
    copies = [
        pltpu.make_async_copy(x_hbm, x_ref, sems.at[0]),
        pltpu.make_async_copy(g_hbm, g_ref, sems.at[1]),
    ]
    for copy in copies:
        copy.start()
    for copy in copies:
        copy.wait()
    x = x_ref[...]
    toks, feats = x.shape
    twice = jnp.concatenate([x, x], axis=0)
    keep = iota(twice.shape, 1) // F == iota(twice.shape, 0) // toks
    twice = jnp.where(keep, twice, jnp.zeros_like(twice))
    pick = jnp.where(iota((F, feats), 1) % F == iota((F, feats), 0), 1.0, 0.0).astype(BF)
    x = dot_last(pick, twice).astype(BF)
    blocks = [jnp.concatenate([x, g_ref[F * h : F * (h + 1)]], axis=0) for h in range(2)]
    for z in range(out_ref.shape[0]):
        out_ref[z] = blocks[z % 2]


def placed(routes, rows, capacity, tokens):
    lanes = routes.shape[1]
    expert = iota((rows, lanes), 0) // capacity
    slot = iota((rows, lanes), 0) % capacity
    first, second = routes[0:1, :] == expert, routes[1:2, :] == expert
    named = first | second
    i, j = iota((lanes, lanes), 0), iota((lanes, lanes), 1)
    earlier = jnp.where((i < tokens) & (i < j % tokens), 1.0, 0.0).astype(BF)
    before = dot(jnp.where(named, 1.0, 0.0).astype(BF), earlier)
    return named & (before == slot.astype(F32)), first, second


def tables_kernel(
    routes_b_ref, gates_b_ref, routes_a_ref, gates_a_ref, picks_b_ref, mix_ref, picks_a_ref, weight_a_ref
):
    def weights(hit, first, second, gates):
        named = jnp.where(first, gates[0:1, :], 0.0) + jnp.where(second, gates[1:2, :], 0.0)
        return jnp.where(hit, named, 0.0)

    routes, gates = routes_b_ref[...], gates_b_ref[...]
    toks = routes.shape[1] // 2
    hit, first, second = placed(routes, picks_b_ref.shape[1], CAP_B, toks)
    lane = iota(hit.shape, 1) // toks
    for h in range(2):
        picks_b_ref[h] = jnp.where(hit & (lane == h), 1.0, 0.0).astype(BF)
    weight = weights(hit, first, second, gates).T[:toks]
    high = weight.astype(BF)
    rest = weight - high.astype(F32)
    middle = rest.astype(BF)
    mix_ref[0] = high
    mix_ref[1] = middle
    mix_ref[2] = (rest - middle.astype(F32)).astype(BF)

    routes, gates = routes_a_ref[...], gates_a_ref[...]
    hit, first, second = placed(routes, picks_a_ref.shape[0], CAP_A, routes.shape[1])
    picks_a_ref[...] = jnp.where(hit, 1.0, 0.0).astype(BF)
    weight = jnp.sum(weights(hit, first, second, gates), axis=1, keepdims=True)
    weight_a_ref[...] = jnp.broadcast_to(weight, weight_a_ref.shape)


def rows_new_kernel(picks_ref, got_ref, out_ref):
    experts, _, slots, width = out_ref.shape
    x = got_ref[:, 0:F, :].reshape(-1, picks_ref.shape[2])
    for h in range(2):
        block = dot_last(picks_ref[h], x).astype(BF).reshape(experts, slots, -1)
        for xh in range(2):
            out_ref[:, xh, :, h * (width // 2) : (h + 1) * (width // 2)] = block


def rows_old_kernel(picks_ref, weight_ref, got_ref, out_ref):
    g = got_ref[:, F : 2 * F, :].reshape(-1, picks_ref.shape[1])
    block = (dot_last(picks_ref[...], g) * weight_ref[:, 0:1]).astype(BF)
    experts, _, slots, width = out_ref.shape
    for xh in range(2):
        out_ref[:, xh] = block.reshape(experts, slots, width)


def up_kernel(own_ref, other_ref, gu_ref, dn_ref, hidden_ref, out_ref):
    total = None
    for o, ref in enumerate((own_ref, other_ref)):
        for xh in range(2):
            term = dot_last(rows_of(ref, xh), gu_ref[o, xh])
            total = term if total is None else total + term
    gate, up = total[:, :128], total[:, 128:]
    hidden = (gate / (1.0 + jnp.exp(-gate)) * up).astype(BF)
    hidden_ref[...] = hidden
    groups, _, slots, width = out_ref.shape
    for xh in range(2):
        out_ref[:, xh] = dot(hidden, dn_ref[1, xh]).astype(BF).reshape(groups, slots, width)


def down_kernel(hidden_ref, dn_ref, arrived_ref, out_ref):
    hidden = hidden_ref[...]
    groups, _, slots, width = out_ref.shape
    for xh in range(2):
        total = dot(hidden, dn_ref[0, xh]) + rows_of(arrived_ref, xh).astype(F32)
        out_ref[:, xh] = total.astype(BF).reshape(groups, slots, width)


def mix_kernel(mix_ref, got_ref, out_ref):
    width = got_ref.shape[3] // 2
    rows = [rows_of(got_ref, xh) for xh in range(2)]
    halves = []
    for h in range(2):
        total = None
        for xh in range(2):
            for part in range(3):
                term = dot(mix_ref[part], rows[xh][:, h * width : (h + 1) * width])
                total = term if total is None else total + term
        halves.append(total)
    mixed = jnp.concatenate(halves, axis=0).T.astype(BF)
    out_ref[...] = mixed.reshape(out_ref.shape)


def total_kernel(got_ref, out_ref):
    total = got_ref[0].astype(F32)
    for z in range(1, got_ref.shape[0]):
        total = total + got_ref[z].astype(F32)
    turned = total.T
    toks = out_ref.shape[0]
    out_ref[...] = jnp.concatenate([turned[:toks], turned[toks:]], axis=1).astype(BF)


def rows_of(ref, xh):
    return ref[:, xh].reshape(-1, ref.shape[3])


def back_kernel(
    me_ref, own_ref, near_ref, other_ref, other_near_ref, dn_ref, gate_ref, up_ref,
    down_ref, dg_ref, du_ref, held,
):
    width = own_ref.shape[3]
    mine = pl.ds(pl.multiple_of(me_ref[1] * width, width), width)
    rest = pl.ds(pl.multiple_of((1 - me_ref[1]) * width, width), width)
    parts = ((0, mine, own_ref), (1, mine, other_ref), (0, rest, near_ref), (1, rest, other_near_ref))
    total = None
    for o, lanes, ref in parts:
        for xh in range(2):
            term = dot_last(dn_ref[o, xh, :, lanes], rows_of(ref, xh))
            total = term if total is None else total + term
    gate, up = gate_ref[...].astype(F32), up_ref[...].astype(F32)
    grad = total[: gate.shape[0]]
    sigma = 1.0 / (1.0 + jnp.exp(-gate))
    active = gate * sigma
    dg_ref[...] = (grad * up * sigma * (1.0 + gate * (1.0 - sigma))).astype(BF)
    du_ref[...] = (grad * active).astype(BF)
    hidden = (active * up).astype(BF)
    for o, lanes, ref in parts:
        for xh in range(2):
            held[o, xh, :, lanes] = dot(hidden, rows_of(ref, xh)).astype(BF)
    order = lane_order(me_ref[0])
    for xh in range(2):
        for zq in range(4):
            tiles = [
                held[o, xh, :, pl.ds(h * 512 + zq * 128, 128)] for o in range(2) for h in range(2)
            ]
            moved = dot_last(jnp.concatenate(tiles, axis=1), order).astype(BF)
            for zi in range(4):
                down_ref[:, pl.ds((zq * 4 + zi) * 256 + xh * 128, 128)] = moved[
                    :, zi * 128 : (zi + 1) * 128
                ]


def other_core(array):
    return lax.ppermute(array, CORE, [(0, 1), (1, 0)])


def exchange(array, axes):
    peers = array.reshape(lax.axis_size(axes), -1, array.shape[-1])
    return lax.all_to_all(peers, axes, 0, 0, tiled=True).reshape(array.shape)


def per_device(
    x_new,
    routes_new,
    gates_new,
    w_gate,
    w_up,
    w_down,
    grad_out,
    routes_old,
    gates_old,
    pre_gate,
    pre_up,
):
    me = jnp.stack([lax.axis_index(CORE), lax.axis_index(Z) % 2]).astype(jnp.int32)
    experts = lax.axis_size(EXPERT)
    rows_new, rows_old = experts * CAP_B, experts * CAP_A
    hidden_units = w_gate.shape[2]
    twice = lambda a: jnp.concatenate([a.T, a.T], axis=1)
    routes_b, gates_b = twice(routes_new), twice(gates_new)
    routes_a, gates_a = routes_old.T, gates_old.T

    packed = pl.pallas_call(
        pack_kernel,
        out_shape=shape(16, 2 * F, 128),
        in_specs=[pl.BlockSpec(memory_space=pltpu.HBM)] * 2,
        out_specs=pl.BlockSpec(memory_space=pltpu.VMEM),
        scratch_shapes=[
            pltpu.VMEM(x_new.shape, BF),
            pltpu.VMEM(grad_out.shape[::-1], BF),
            pltpu.SemaphoreType.DMA((2,)),
        ],
        compiler_params=pltpu.CompilerParams(vmem_limit_bytes=16 * MIB),
        name="pack_kernel",
    )(x_new, grad_out.T)
    got = lax.all_to_all(packed, Z, 0, 0, tiled=True)
    gate_up, down = call(
        weights_kernel,
        (shape(2, 2, 256, 1024), shape(2, 2, 128, 1024)),
        me,
        w_gate[0].T,
        w_up[0].T,
        w_down[0],
        scalars=1,
        flops=14 * 10**8,
        moved=6 * 10**6,
    )

    picks_b, mix, picks_a, weight_a = call(
        tables_kernel,
        (
            shape(2, rows_new, 128),
            shape(3, x_new.shape[0], rows_new),
            shape(rows_old, 128),
            shape(rows_old, 128, dtype=F32),
        ),
        routes_b,
        gates_b,
        routes_a,
        gates_a,
    )
    got, gate_up, down, picks_b, mix, picks_a, weight_a = lax.optimization_barrier(
        (got, gate_up, down, picks_b, mix, picks_a, weight_a)
    )

    rows_b = shape(experts, 2, CAP_B, 1024)
    own = exchange(call(rows_new_kernel, rows_b, picks_b, got), PLANE)
    rows_a = shape(experts, 2, CAP_A, 512)
    sent_a = call(rows_old_kernel, rows_a, picks_a, weight_a, got)
    own, sent_a = lax.optimization_barrier((own, sent_a))
    own_a = exchange(sent_a, PLANE)

    hidden, partial = call(
        up_kernel,
        (shape(rows_new, 128), rows_b),
        own,
        other_core(own),
        gate_up,
        down,
        flops=8 * 10**8,
        moved=4 * 10**6,
    )
    summed = call(down_kernel, rows_b, hidden, down, other_core(partial), flops=2 * 10**8)
    returned = exchange(summed, PLANE)

    near_a = lax.ppermute(own_a, Z, [(z, z ^ 1) for z in range(lax.axis_size(Z))])
    other_a, other_near = other_core(own_a), other_core(near_a)
    vmem = pl.BlockSpec(memory_space=pltpu.VMEM)
    weight_grad, gate_grad, up_grad = pl.pallas_call(
        back_kernel,
        out_shape=(
            shape(hidden_units, 4096),
            shape(hidden_units, rows_old),
            shape(hidden_units, rows_old),
        ),
        in_specs=[pl.BlockSpec(memory_space=pltpu.SMEM)] + [vmem] * 7,
        out_specs=(vmem,) * 3,
        scratch_shapes=[pltpu.VMEM((2, 2, hidden_units, 1024), BF)],
        cost_estimate=pl.CostEstimate(
            flops=15 * 10**8, bytes_accessed=8 * 10**6, transcendentals=0
        ),
        compiler_params=pltpu.CompilerParams(vmem_limit_bytes=16 * MIB),
        name="back_kernel",
    )(me, own_a, near_a, other_a, other_near, down, pre_gate[0].T, pre_up[0].T)
    mixed = call(mix_kernel, shape(16, F, 128), mix, returned, flops=4 * 10**8)
    mixed = exchange(mixed, Z)
    mixed, weight_grad, gate_grad, up_grad = lax.optimization_barrier(
        (mixed, weight_grad, gate_grad, up_grad)
    )
    mixed = call(total_kernel, shape(*x_new.shape), mixed)
    return (mixed, weight_grad[None], gate_grad.T[None], up_grad.T[None])


def solution(mesh):
    torus = Mesh(
        mesh.devices.reshape(4, 2, 16, 2, 2), ("expert_0", "expert_1", "dp_0", "dp_1", "dp_2")
    )
    placed_as = (
        P(EXPERT, DP),
        P(EXPERT, None),
        P(EXPERT, None),
        P(EXPERT, None, DP),
        P(EXPERT, None, DP),
        P(EXPERT, DP, None),
        P(EXPERT, DP),
        P(EXPERT, None),
        P(EXPERT, None),
        P(EXPERT, None, DP),
        P(EXPERT, None, DP),
    )
    return jax.shard_map(
        per_device,
        mesh=torus,
        in_specs=placed_as,
        out_specs=(P(EXPERT, DP), P(EXPERT, DP, None), P(EXPERT, None, DP), P(EXPERT, None, DP)),
        check_vma=False,
    )
```

```python
import functools

import jax
import jax.numpy as jnp
from jax import lax
from jax.experimental import pallas as pl
from jax.experimental.pallas import tpu as pltpu
from jax.sharding import Mesh
from jax.sharding import PartitionSpec as P

CAP_B = 32
CAP_A = 64
EXPERT = ("expert_0", "expert_1")
DP = ("dp_0", "dp_1", "dp_2")
Z = "dp_0"
CORE = "dp_2"
PLANE = ("expert_0", "expert_1", "dp_1")
F = 32
BF = jnp.bfloat16
F32 = jnp.float32
LAST = (((1,), (1,)), ((), ()))
MIB = 1 << 20


def iota(shape, dim):
    return lax.broadcasted_iota(jnp.int32, shape, dim)


def dot(a, b):
    return jnp.dot(a, b, preferred_element_type=F32)


def dot_last(a, b):
    return lax.dot_general(a, b, LAST, preferred_element_type=F32)


def call(body, outs, *args, flops=10**7, moved=10**6, scalars=0):
    vmem = pl.BlockSpec(memory_space=pltpu.VMEM)
    smem = pl.BlockSpec(memory_space=pltpu.SMEM)
    many = isinstance(outs, (tuple, list))
    return pl.pallas_call(
        body,
        out_shape=outs,
        in_specs=[smem] * scalars + [vmem] * (len(args) - scalars),
        out_specs=tuple(vmem for _ in outs) if many else vmem,
        cost_estimate=pl.CostEstimate(flops=flops, bytes_accessed=moved, transcendentals=0),
        compiler_params=pltpu.CompilerParams(vmem_limit_bytes=16 * MIB),
        name=body.__name__,
    )(*args)


def shape(*dims, dtype=BF):
    return jax.ShapeDtypeStruct(dims, dtype)


def lane_order(me):
    i, j = iota((512, 512), 0), iota((512, 512), 1)
    core = jnp.bitwise_xor((i // 64) % 2, me)
    hit = (
        (i // 128 == (j // F) % 4)
        & (core == j // 256)
        & ((i // F) % 2 == (j // 128) % 2)
        & (i % F == j % F)
    )
    return jnp.where(hit, 1.0, 0.0).astype(BF)


def weights_kernel(me_ref, gate_ref, up_ref, down_ref, gu_ref, dn_ref):
    order = lane_order(me_ref[0])
    gu_ref[...] = jnp.zeros_like(gu_ref)
    dn_ref[...] = jnp.zeros_like(dn_ref)
    hidden = gate_ref.shape[0]
    for ref, out, base in ((gate_ref, gu_ref, 0), (up_ref, gu_ref, 128), (down_ref, dn_ref, 0)):
        for xh in range(2):
            for zq in range(4):
                tiles = [
                    ref[:, pl.ds((zq * 4 + zi) * 256 + xh * 128, 128)] for zi in range(4)
                ]
                moved = dot(jnp.concatenate(tiles, axis=1), order).astype(BF)
                for o in range(2):
                    for h in range(2):
                        out[o, xh, pl.ds(base, hidden), pl.ds(h * 512 + zq * 128, 128)] = moved[
                            :, (o * 2 + h) * 128 : (o * 2 + h + 1) * 128
                        ]


def pack_kernel(x_hbm, g_hbm, out_ref, x_ref, g_ref, sems):
    copies = [
        pltpu.make_async_copy(x_hbm, x_ref, sems.at[0]),
        pltpu.make_async_copy(g_hbm, g_ref, sems.at[1]),
    ]
    for copy in copies:
        copy.start()
    for copy in copies:
        copy.wait()
    x = x_ref[...]
    toks, feats = x.shape
    twice = jnp.concatenate([x, x], axis=0)
    keep = iota(twice.shape, 1) // F == iota(twice.shape, 0) // toks
    twice = jnp.where(keep, twice, jnp.zeros_like(twice))
    pick = jnp.where(iota((F, feats), 1) % F == iota((F, feats), 0), 1.0, 0.0).astype(BF)
    x = dot_last(pick, twice).astype(BF)
    blocks = [jnp.concatenate([x, g_ref[F * h : F * (h + 1)]], axis=0) for h in range(2)]
    for z in range(out_ref.shape[0]):
        out_ref[z] = blocks[z % 2]


def placed(routes, rows, capacity, tokens):
    lanes = routes.shape[1]
    expert = iota((rows, lanes), 0) // capacity
    slot = iota((rows, lanes), 0) % capacity
    first, second = routes[0:1, :] == expert, routes[1:2, :] == expert
    named = first | second
    i, j = iota((lanes, lanes), 0), iota((lanes, lanes), 1)
    earlier = jnp.where((i < tokens) & (i < j % tokens), 1.0, 0.0).astype(BF)
    before = dot(jnp.where(named, 1.0, 0.0).astype(BF), earlier)
    return named & (before == slot.astype(F32)), first, second


def tables_kernel(
    routes_b_ref, gates_b_ref, routes_a_ref, gates_a_ref, picks_b_ref, mix_ref, picks_a_ref, weight_a_ref
):
    def weights(hit, first, second, gates):
        named = jnp.where(first, gates[0:1, :], 0.0) + jnp.where(second, gates[1:2, :], 0.0)
        return jnp.where(hit, named, 0.0)

    routes, gates = routes_b_ref[...], gates_b_ref[...]
    toks = routes.shape[1] // 2
    hit, first, second = placed(routes, picks_b_ref.shape[1], CAP_B, toks)
    lane = iota(hit.shape, 1) // toks
    for h in range(2):
        picks_b_ref[h] = jnp.where(hit & (lane == h), 1.0, 0.0).astype(BF)
    weight = weights(hit, first, second, gates).T[:toks]
    high = weight.astype(BF)
    rest = weight - high.astype(F32)
    middle = rest.astype(BF)
    mix_ref[0] = high
    mix_ref[1] = middle
    mix_ref[2] = (rest - middle.astype(F32)).astype(BF)

    routes, gates = routes_a_ref[...], gates_a_ref[...]
    hit, first, second = placed(routes, picks_a_ref.shape[0], CAP_A, routes.shape[1])
    picks_a_ref[...] = jnp.where(hit, 1.0, 0.0).astype(BF)
    weight = jnp.sum(weights(hit, first, second, gates), axis=1, keepdims=True)
    weight_a_ref[...] = jnp.broadcast_to(weight, weight_a_ref.shape)


def rows_kernel(picks_b_ref, picks_a_ref, weight_ref, got_ref, out_ref):
    experts, _, both, width = out_ref.shape
    slots, half = both // 2, width // 2
    x = got_ref[:, 0:F, :].reshape(-1, picks_b_ref.shape[2])
    for h in range(2):
        block = dot_last(picks_b_ref[h], x).astype(BF).reshape(experts, slots, half)
        for xh in range(2):
            out_ref[:, xh, :slots, h * half : (h + 1) * half] = block
    g = got_ref[:, F : 2 * F, :].reshape(-1, picks_a_ref.shape[1])
    block = (dot_last(picks_a_ref[...], g) * weight_ref[:, 0:1]).astype(BF)
    block = block.reshape(experts, 2 * slots, half)
    for xh in range(2):
        out_ref[:, xh, slots:, :half] = block[:, :slots]
        out_ref[:, xh, slots:, half:] = block[:, slots:]


def up_kernel(own_ref, other_ref, gu_ref, dn_ref, hidden_ref, out_ref):
    total = None
    for o, ref in enumerate((own_ref, other_ref)):
        for xh in range(2):
            term = dot_last(rows_of(ref, xh), gu_ref[o, xh])
            total = term if total is None else total + term
    gate, up = total[:, :128], total[:, 128:]
    hidden = (gate / (1.0 + jnp.exp(-gate)) * up).astype(BF)
    hidden_ref[...] = hidden
    groups, _, slots, width = out_ref.shape
    for xh in range(2):
        out_ref[:, xh] = dot(hidden, dn_ref[1, xh]).astype(BF).reshape(groups, slots, width)


def down_kernel(hidden_ref, dn_ref, arrived_ref, out_ref):
    hidden = hidden_ref[...]
    groups, _, slots, width = out_ref.shape
    for xh in range(2):
        total = dot(hidden, dn_ref[0, xh]) + rows_of(arrived_ref, xh).astype(F32)
        out_ref[:, xh] = total.astype(BF).reshape(groups, slots, width)


def mix_kernel(mix_ref, got_ref, out_ref):
    width = got_ref.shape[3] // 2
    rows = [rows_of(got_ref, xh) for xh in range(2)]
    halves = []
    for h in range(2):
        total = None
        for xh in range(2):
            for part in range(3):
                term = dot(mix_ref[part], rows[xh][:, h * width : (h + 1) * width])
                total = term if total is None else total + term
        halves.append(total)
    mixed = jnp.concatenate(halves, axis=0).T.astype(BF)
    out_ref[...] = mixed.reshape(out_ref.shape)


def total_kernel(got_ref, out_ref):
    total = got_ref[0].astype(F32)
    for z in range(1, got_ref.shape[0]):
        total = total + got_ref[z].astype(F32)
    turned = total.T
    toks = out_ref.shape[0]
    out_ref[...] = jnp.concatenate([turned[:toks], turned[toks:]], axis=1).astype(BF)


def rows_of(ref, xh):
    return ref[:, xh].reshape(-1, ref.shape[3])


def half_rows_of(ref, xh):
    half = ref.shape[3] // 2
    both = jnp.concatenate([ref[:, xh, :, :half], ref[:, xh, :, half:]], axis=1)
    return both.reshape(-1, half)


def back_kernel(
    me_ref, own_ref, near_ref, other_ref, other_near_ref, dn_ref, gate_ref, up_ref,
    down_ref, dg_ref, du_ref, held,
):
    width = own_ref.shape[3] // 2
    mine = pl.ds(pl.multiple_of(me_ref[1] * width, width), width)
    rest = pl.ds(pl.multiple_of((1 - me_ref[1]) * width, width), width)
    parts = ((0, mine, own_ref), (1, mine, other_ref), (0, rest, near_ref), (1, rest, other_near_ref))
    total = None
    for o, lanes, ref in parts:
        for xh in range(2):
            term = dot_last(dn_ref[o, xh, :, lanes], half_rows_of(ref, xh))
            total = term if total is None else total + term
    gate, up = gate_ref[...].astype(F32), up_ref[...].astype(F32)
    grad = total[: gate.shape[0]]
    sigma = 1.0 / (1.0 + jnp.exp(-gate))
    active = gate * sigma
    dg_ref[...] = (grad * up * sigma * (1.0 + gate * (1.0 - sigma))).astype(BF)
    du_ref[...] = (grad * active).astype(BF)
    hidden = (active * up).astype(BF)
    for o, lanes, ref in parts:
        for xh in range(2):
            held[o, xh, :, lanes] = dot(hidden, half_rows_of(ref, xh)).astype(BF)
    order = lane_order(me_ref[0])
    for xh in range(2):
        for zq in range(4):
            tiles = [
                held[o, xh, :, pl.ds(h * 512 + zq * 128, 128)] for o in range(2) for h in range(2)
            ]
            moved = dot_last(jnp.concatenate(tiles, axis=1), order).astype(BF)
            for zi in range(4):
                down_ref[:, pl.ds((zq * 4 + zi) * 256 + xh * 128, 128)] = moved[
                    :, zi * 128 : (zi + 1) * 128
                ]


def other_core(array):
    return lax.ppermute(array, CORE, [(0, 1), (1, 0)])


def exchange(array, axes):
    peers = array.reshape(lax.axis_size(axes), -1, array.shape[-1])
    return lax.all_to_all(peers, axes, 0, 0, tiled=True).reshape(array.shape)


def per_device(
    x_new,
    routes_new,
    gates_new,
    w_gate,
    w_up,
    w_down,
    grad_out,
    routes_old,
    gates_old,
    pre_gate,
    pre_up,
):
    me = jnp.stack([lax.axis_index(CORE), lax.axis_index(Z) % 2]).astype(jnp.int32)
    experts = lax.axis_size(EXPERT)
    rows_new, rows_old = experts * CAP_B, experts * CAP_A
    hidden_units = w_gate.shape[2]
    twice = lambda a: jnp.concatenate([a.T, a.T], axis=1)
    routes_b, gates_b = twice(routes_new), twice(gates_new)
    routes_a, gates_a = routes_old.T, gates_old.T

    packed = pl.pallas_call(
        pack_kernel,
        out_shape=shape(16, 2 * F, 128),
        in_specs=[pl.BlockSpec(memory_space=pltpu.HBM)] * 2,
        out_specs=pl.BlockSpec(memory_space=pltpu.VMEM),
        scratch_shapes=[
            pltpu.VMEM(x_new.shape, BF),
            pltpu.VMEM(grad_out.shape[::-1], BF),
            pltpu.SemaphoreType.DMA((2,)),
        ],
        compiler_params=pltpu.CompilerParams(vmem_limit_bytes=16 * MIB),
        name="pack_kernel",
    )(x_new, grad_out.T)
    got = lax.all_to_all(packed, Z, 0, 0, tiled=True)
    gate_up, down = call(
        weights_kernel,
        (shape(2, 2, 256, 1024), shape(2, 2, 128, 1024)),
        me,
        w_gate[0].T,
        w_up[0].T,
        w_down[0],
        scalars=1,
        flops=14 * 10**8,
        moved=6 * 10**6,
    )

    picks_b, mix, picks_a, weight_a = call(
        tables_kernel,
        (
            shape(2, rows_new, 128),
            shape(3, x_new.shape[0], rows_new),
            shape(rows_old, 128),
            shape(rows_old, 128, dtype=F32),
        ),
        routes_b,
        gates_b,
        routes_a,
        gates_a,
    )
    got, gate_up, down, picks_b, mix, picks_a, weight_a = lax.optimization_barrier(
        (got, gate_up, down, picks_b, mix, picks_a, weight_a)
    )

    rows_b = shape(experts, 2, CAP_B, 1024)
    sent = call(rows_kernel, shape(experts, 2, 2 * CAP_B, 1024), picks_b, picks_a, weight_a, got)
    arrived = exchange(sent, PLANE)
    own, own_a = arrived[:, :, :CAP_B], arrived[:, :, CAP_B:]

    hidden, partial = call(
        up_kernel,
        (shape(rows_new, 128), rows_b),
        own,
        other_core(own),
        gate_up,
        down,
        flops=8 * 10**8,
        moved=4 * 10**6,
    )
    summed = call(down_kernel, rows_b, hidden, down, other_core(partial), flops=2 * 10**8)
    returned = exchange(summed, PLANE)

    near_a = lax.ppermute(own_a, Z, [(z, z ^ 1) for z in range(lax.axis_size(Z))])
    other_a, other_near = other_core(own_a), other_core(near_a)
    vmem = pl.BlockSpec(memory_space=pltpu.VMEM)
    weight_grad, gate_grad, up_grad = pl.pallas_call(
        back_kernel,
        out_shape=(
            shape(hidden_units, 4096),
            shape(hidden_units, rows_old),
            shape(hidden_units, rows_old),
        ),
        in_specs=[pl.BlockSpec(memory_space=pltpu.SMEM)] + [vmem] * 7,
        out_specs=(vmem,) * 3,
        scratch_shapes=[pltpu.VMEM((2, 2, hidden_units, 1024), BF)],
        cost_estimate=pl.CostEstimate(
            flops=15 * 10**8, bytes_accessed=8 * 10**6, transcendentals=0
        ),
        compiler_params=pltpu.CompilerParams(vmem_limit_bytes=16 * MIB),
        name="back_kernel",
    )(me, own_a, near_a, other_a, other_near, down, pre_gate[0].T, pre_up[0].T)
    mixed = call(mix_kernel, shape(16, F, 128), mix, returned, flops=4 * 10**8)
    mixed = exchange(mixed, Z)
    mixed, weight_grad, gate_grad, up_grad = lax.optimization_barrier(
        (mixed, weight_grad, gate_grad, up_grad)
    )
    mixed = call(total_kernel, shape(*x_new.shape), mixed)
    return (mixed, weight_grad[None], gate_grad.T[None], up_grad.T[None])


def solution(mesh):
    torus = Mesh(
        mesh.devices.reshape(4, 2, 16, 2, 2), ("expert_0", "expert_1", "dp_0", "dp_1", "dp_2")
    )
    placed_as = (
        P(EXPERT, DP),
        P(EXPERT, None),
        P(EXPERT, None),
        P(EXPERT, None, DP),
        P(EXPERT, None, DP),
        P(EXPERT, DP, None),
        P(EXPERT, DP),
        P(EXPERT, None),
        P(EXPERT, None),
        P(EXPERT, None, DP),
        P(EXPERT, None, DP),
    )
    return jax.shard_map(
        per_device,
        mesh=torus,
        in_specs=placed_as,
        out_specs=(P(EXPERT, DP), P(EXPERT, DP, None), P(EXPERT, None, DP), P(EXPERT, None, DP)),
        check_vma=False,
    )
```

```python
import functools

import jax
import jax.numpy as jnp
from jax import lax
from jax.experimental import pallas as pl
from jax.experimental.pallas import tpu as pltpu
from jax.sharding import Mesh
from jax.sharding import PartitionSpec as P

CAP_B = 32
CAP_A = 64
EXPERT = ("expert_0", "expert_1")
DP = ("dp_0", "dp_1", "dp_2")
Z = "dp_0"
CORE = "dp_2"
PLANE = ("expert_0", "expert_1", "dp_1")
F = 32
BF = jnp.bfloat16
F32 = jnp.float32
LAST = (((1,), (1,)), ((), ()))
MIB = 1 << 20


def iota(shape, dim):
    return lax.broadcasted_iota(jnp.int32, shape, dim)


def dot(a, b):
    return jnp.dot(a, b, preferred_element_type=F32)


def dot_last(a, b):
    return lax.dot_general(a, b, LAST, preferred_element_type=F32)


def call(body, outs, *args, flops=10**7, moved=10**6, scalars=0):
    vmem = pl.BlockSpec(memory_space=pltpu.VMEM)
    smem = pl.BlockSpec(memory_space=pltpu.SMEM)
    many = isinstance(outs, (tuple, list))
    return pl.pallas_call(
        body,
        out_shape=outs,
        in_specs=[smem] * scalars + [vmem] * (len(args) - scalars),
        out_specs=tuple(vmem for _ in outs) if many else vmem,
        cost_estimate=pl.CostEstimate(flops=flops, bytes_accessed=moved, transcendentals=0),
        compiler_params=pltpu.CompilerParams(vmem_limit_bytes=16 * MIB),
        name=body.__name__,
    )(*args)


def shape(*dims, dtype=BF):
    return jax.ShapeDtypeStruct(dims, dtype)


def lane_order(me):
    i, j = iota((512, 512), 0), iota((512, 512), 1)
    core = jnp.bitwise_xor((i // 64) % 2, me)
    hit = (
        (i // 128 == (j // F) % 4)
        & (core == j // 256)
        & ((i // F) % 2 == (j // 128) % 2)
        & (i % F == j % F)
    )
    return jnp.where(hit, 1.0, 0.0).astype(BF)


def weights_kernel(me_ref, gate_ref, up_ref, down_ref, gu_ref, dn_ref):
    order = lane_order(me_ref[0])
    gu_ref[...] = jnp.zeros_like(gu_ref)
    dn_ref[...] = jnp.zeros_like(dn_ref)
    hidden = gate_ref.shape[0]
    for ref, out, base in ((gate_ref, gu_ref, 0), (up_ref, gu_ref, 128), (down_ref, dn_ref, 0)):
        for xh in range(2):
            for zq in range(4):
                tiles = [
                    ref[:, pl.ds((zq * 4 + zi) * 256 + xh * 128, 128)] for zi in range(4)
                ]
                moved = dot(jnp.concatenate(tiles, axis=1), order).astype(BF)
                for o in range(2):
                    for h in range(2):
                        out[o, xh, pl.ds(base, hidden), pl.ds(h * 512 + zq * 128, 128)] = moved[
                            :, (o * 2 + h) * 128 : (o * 2 + h + 1) * 128
                        ]


def pack_kernel(x_hbm, g_hbm, out_ref, x_ref, g_ref, sems):
    copies = [
        pltpu.make_async_copy(x_hbm, x_ref, sems.at[0]),
        pltpu.make_async_copy(g_hbm, g_ref, sems.at[1]),
    ]
    for copy in copies:
        copy.start()
    for copy in copies:
        copy.wait()
    x = x_ref[...]
    toks, feats = x.shape
    twice = jnp.concatenate([x, x], axis=0)
    keep = iota(twice.shape, 1) // F == iota(twice.shape, 0) // toks
    twice = jnp.where(keep, twice, jnp.zeros_like(twice))
    pick = jnp.where(iota((F, feats), 1) % F == iota((F, feats), 0), 1.0, 0.0).astype(BF)
    x = dot_last(pick, twice).astype(BF)
    blocks = [jnp.concatenate([x, g_ref[F * h : F * (h + 1)]], axis=0) for h in range(2)]
    for z in range(out_ref.shape[0]):
        out_ref[z] = blocks[z % 2]


def placed(routes, rows, capacity, tokens):
    lanes = routes.shape[1]
    expert = iota((rows, lanes), 0) // capacity
    slot = iota((rows, lanes), 0) % capacity
    first, second = routes[0:1, :] == expert, routes[1:2, :] == expert
    named = first | second
    i, j = iota((lanes, lanes), 0), iota((lanes, lanes), 1)
    earlier = jnp.where((i < tokens) & (i < j % tokens), 1.0, 0.0).astype(BF)
    before = dot(jnp.where(named, 1.0, 0.0).astype(BF), earlier)
    return named & (before == slot.astype(F32)), first, second


def named_weights(hit, first, second, gates):
    named = jnp.where(first, gates[0:1, :], 0.0) + jnp.where(second, gates[1:2, :], 0.0)
    return jnp.where(hit, named, 0.0)


def tables_kernel(routes_ref, gates_ref, picks_ref, mix_ref):
    routes, gates = routes_ref[...], gates_ref[...]
    toks = routes.shape[1] // 2
    hit, first, second = placed(routes, picks_ref.shape[1], CAP_B, toks)
    lane = iota(hit.shape, 1) // toks
    for h in range(2):
        picks_ref[h] = jnp.where(hit & (lane == h), 1.0, 0.0).astype(BF)
    weight = named_weights(hit, first, second, gates).T[:toks]
    high = weight.astype(BF)
    rest = weight - high.astype(F32)
    middle = rest.astype(BF)
    mix_ref[0] = high
    mix_ref[1] = middle
    mix_ref[2] = (rest - middle.astype(F32)).astype(BF)


def rows_kernel(picks_ref, routes_ref, gates_ref, got_ref, out_ref):
    experts, _, both, width = out_ref.shape
    slots, half = both // 2, width // 2
    x = got_ref[:, 0:F, :].reshape(-1, picks_ref.shape[2])
    for h in range(2):
        block = dot_last(picks_ref[h], x).astype(BF).reshape(experts, slots, half)
        for xh in range(2):
            out_ref[:, xh, :slots, h * half : (h + 1) * half] = block
    routes, gates = routes_ref[...], gates_ref[...]
    toks = routes.shape[1]
    hit, first, second = placed(routes, experts * 2 * slots, 2 * slots, toks)
    weight = jnp.sum(named_weights(hit, first, second, gates), axis=1, keepdims=True)
    g = got_ref[:, F : 2 * F, :].reshape(-1, toks)
    block = (dot_last(jnp.where(hit, 1.0, 0.0).astype(BF), g) * weight).astype(BF)
    block = block.reshape(experts, 2 * slots, half)
    for xh in range(2):
        out_ref[:, xh, slots:, :half] = block[:, :slots]
        out_ref[:, xh, slots:, half:] = block[:, slots:]


def up_kernel(own_ref, other_ref, gu_ref, dn_ref, hidden_ref, out_ref):
    total = None
    for o, ref in enumerate((own_ref, other_ref)):
        for xh in range(2):
            term = dot_last(rows_of(ref, xh), gu_ref[o, xh])
            total = term if total is None else total + term
    gate, up = total[:, :128], total[:, 128:]
    hidden = (gate / (1.0 + jnp.exp(-gate)) * up).astype(BF)
    hidden_ref[...] = hidden
    groups, _, slots, width = out_ref.shape
    for xh in range(2):
        out_ref[:, xh] = dot(hidden, dn_ref[1, xh]).astype(BF).reshape(groups, slots, width)


def down_kernel(hidden_ref, dn_ref, arrived_ref, out_ref):
    hidden = hidden_ref[...]
    groups, _, slots, width = out_ref.shape
    for xh in range(2):
        total = dot(hidden, dn_ref[0, xh]) + rows_of(arrived_ref, xh).astype(F32)
        out_ref[:, xh] = total.astype(BF).reshape(groups, slots, width)


def mix_kernel(mix_ref, got_ref, out_ref):
    width = got_ref.shape[3] // 2
    parts, toks, rows = mix_ref.shape
    mix = mix_ref[...].reshape(parts * toks, rows)
    halves = []
    for h in range(2):
        total = sum(dot(mix, rows_of(got_ref, xh)[:, h * width : (h + 1) * width]) for xh in range(2))
        halves.append(total[:toks] + total[toks : 2 * toks] + total[2 * toks :])
    mixed = jnp.concatenate(halves, axis=0).T.astype(BF)
    out_ref[...] = mixed.reshape(out_ref.shape)


def total_kernel(got_ref, out_ref):
    total = got_ref[0].astype(F32)
    for z in range(1, got_ref.shape[0]):
        total = total + got_ref[z].astype(F32)
    turned = total.T
    toks = out_ref.shape[0]
    out_ref[...] = jnp.concatenate([turned[:toks], turned[toks:]], axis=1).astype(BF)


def rows_of(ref, xh):
    return ref[:, xh].reshape(-1, ref.shape[3])


def half_rows_of(ref, xh):
    half = ref.shape[3] // 2
    both = jnp.concatenate([ref[:, xh, :, :half], ref[:, xh, :, half:]], axis=1)
    return both.reshape(-1, half)


def back_kernel(
    me_ref, own_ref, near_ref, other_ref, other_near_ref, dn_ref, gate_ref, up_ref,
    down_ref, dg_ref, du_ref, held,
):
    width = own_ref.shape[3] // 2
    mine = pl.ds(pl.multiple_of(me_ref[1] * width, width), width)
    rest = pl.ds(pl.multiple_of((1 - me_ref[1]) * width, width), width)
    parts = ((0, mine, own_ref), (1, mine, other_ref), (0, rest, near_ref), (1, rest, other_near_ref))
    total = None
    for o, lanes, ref in parts:
        for xh in range(2):
            term = dot_last(dn_ref[o, xh, :, lanes], half_rows_of(ref, xh))
            total = term if total is None else total + term
    gate, up = gate_ref[...].astype(F32), up_ref[...].astype(F32)
    grad = total[: gate.shape[0]]
    sigma = 1.0 / (1.0 + jnp.exp(-gate))
    active = gate * sigma
    dg_ref[...] = (grad * up * sigma * (1.0 + gate * (1.0 - sigma))).astype(BF)
    du_ref[...] = (grad * active).astype(BF)
    hidden = (active * up).astype(BF)
    for o, lanes, ref in parts:
        for xh in range(2):
            held[o, xh, :, lanes] = dot(hidden, half_rows_of(ref, xh)).astype(BF)
    order = lane_order(me_ref[0])
    for xh in range(2):
        for zq in range(4):
            tiles = [
                held[o, xh, :, pl.ds(h * 512 + zq * 128, 128)] for o in range(2) for h in range(2)
            ]
            moved = dot_last(jnp.concatenate(tiles, axis=1), order).astype(BF)
            for zi in range(4):
                down_ref[:, pl.ds((zq * 4 + zi) * 256 + xh * 128, 128)] = moved[
                    :, zi * 128 : (zi + 1) * 128
                ]


def other_core(array):
    return lax.ppermute(array, CORE, [(0, 1), (1, 0)])


def exchange(array, axes):
    peers = array.reshape(lax.axis_size(axes), -1, array.shape[-1])
    return lax.all_to_all(peers, axes, 0, 0, tiled=True).reshape(array.shape)


def per_device(
    x_new,
    routes_new,
    gates_new,
    w_gate,
    w_up,
    w_down,
    grad_out,
    routes_old,
    gates_old,
    pre_gate,
    pre_up,
):
    me = jnp.stack([lax.axis_index(CORE), lax.axis_index(Z) % 2]).astype(jnp.int32)
    experts = lax.axis_size(EXPERT)
    rows_new, rows_old = experts * CAP_B, experts * CAP_A
    hidden_units = w_gate.shape[2]
    twice = lambda a: jnp.concatenate([a.T, a.T], axis=1)
    routes_b, gates_b = twice(routes_new), twice(gates_new)
    routes_a, gates_a = routes_old.T, gates_old.T

    packed = pl.pallas_call(
        pack_kernel,
        out_shape=shape(16, 2 * F, 128),
        in_specs=[pl.BlockSpec(memory_space=pltpu.HBM)] * 2,
        out_specs=pl.BlockSpec(memory_space=pltpu.VMEM),
        scratch_shapes=[
            pltpu.VMEM(x_new.shape, BF),
            pltpu.VMEM(grad_out.shape[::-1], BF),
            pltpu.SemaphoreType.DMA((2,)),
        ],
        compiler_params=pltpu.CompilerParams(vmem_limit_bytes=16 * MIB),
        name="pack_kernel",
    )(x_new, grad_out.T)
    got = lax.all_to_all(packed, Z, 0, 0, tiled=True)
    gate_up, down = call(
        weights_kernel,
        (shape(2, 2, 256, 1024), shape(2, 2, 128, 1024)),
        me,
        w_gate[0].T,
        w_up[0].T,
        w_down[0],
        scalars=1,
        flops=14 * 10**8,
        moved=6 * 10**6,
    )

    picks, mix = call(
        tables_kernel,
        (shape(2, rows_new, 128), shape(3, x_new.shape[0], rows_new)),
        routes_b,
        gates_b,
    )
    got, gate_up, down, picks, mix, routes_a, gates_a = lax.optimization_barrier(
        (got, gate_up, down, picks, mix, routes_a, gates_a)
    )

    rows_b = shape(experts, 2, CAP_B, 1024)
    sent = call(
        rows_kernel, shape(experts, 2, 2 * CAP_B, 1024), picks, routes_a, gates_a, got
    )
    arrived = exchange(sent, PLANE)
    own, own_a = arrived[:, :, :CAP_B], arrived[:, :, CAP_B:]

    hidden, partial = call(
        up_kernel,
        (shape(rows_new, 128), rows_b),
        own,
        other_core(own),
        gate_up,
        down,
        flops=8 * 10**8,
        moved=4 * 10**6,
    )
    summed = call(down_kernel, rows_b, hidden, down, other_core(partial), flops=2 * 10**8)
    returned = exchange(summed, PLANE)

    near_a = lax.ppermute(own_a, Z, [(z, z ^ 1) for z in range(lax.axis_size(Z))])
    other_a, other_near = other_core(own_a), other_core(near_a)
    vmem = pl.BlockSpec(memory_space=pltpu.VMEM)
    weight_grad, gate_grad, up_grad = pl.pallas_call(
        back_kernel,
        out_shape=(
            shape(hidden_units, 4096),
            shape(hidden_units, rows_old),
            shape(hidden_units, rows_old),
        ),
        in_specs=[pl.BlockSpec(memory_space=pltpu.SMEM)] + [vmem] * 7,
        out_specs=(vmem,) * 3,
        scratch_shapes=[pltpu.VMEM((2, 2, hidden_units, 1024), BF)],
        cost_estimate=pl.CostEstimate(
            flops=15 * 10**8, bytes_accessed=8 * 10**6, transcendentals=0
        ),
        compiler_params=pltpu.CompilerParams(vmem_limit_bytes=16 * MIB),
        name="back_kernel",
    )(me, own_a, near_a, other_a, other_near, down, pre_gate[0].T, pre_up[0].T)
    mixed = call(mix_kernel, shape(16, F, 128), mix, returned, flops=4 * 10**8)
    mixed = exchange(mixed, Z)
    mixed, weight_grad, gate_grad, up_grad = lax.optimization_barrier(
        (mixed, weight_grad, gate_grad, up_grad)
    )
    mixed = call(total_kernel, shape(*x_new.shape), mixed)
    return (mixed, weight_grad[None], gate_grad.T[None], up_grad.T[None])


def solution(mesh):
    torus = Mesh(
        mesh.devices.reshape(4, 2, 16, 2, 2), ("expert_0", "expert_1", "dp_0", "dp_1", "dp_2")
    )
    placed_as = (
        P(EXPERT, DP),
        P(EXPERT, None),
        P(EXPERT, None),
        P(EXPERT, None, DP),
        P(EXPERT, None, DP),
        P(EXPERT, DP, None),
        P(EXPERT, DP),
        P(EXPERT, None),
        P(EXPERT, None),
        P(EXPERT, None, DP),
        P(EXPERT, None, DP),
    )
    return jax.shard_map(
        per_device,
        mesh=torus,
        in_specs=placed_as,
        out_specs=(P(EXPERT, DP), P(EXPERT, DP, None), P(EXPERT, None, DP), P(EXPERT, None, DP)),
        check_vma=False,
    )
```

```python
import functools

import jax
import jax.numpy as jnp
from jax import lax
from jax.experimental import pallas as pl
from jax.experimental.pallas import tpu as pltpu
from jax.sharding import Mesh
from jax.sharding import PartitionSpec as P

CAP_B = 32
CAP_A = 64
EXPERT = ("expert_0", "expert_1")
DP = ("dp_0", "dp_1", "dp_2")
Z = "dp_0"
CORE = "dp_2"
PLANE = ("expert_0", "expert_1", "dp_1")
F = 32
BF = jnp.bfloat16
F32 = jnp.float32
LAST = (((1,), (1,)), ((), ()))
MIB = 1 << 20


def iota(shape, dim):
    return lax.broadcasted_iota(jnp.int32, shape, dim)


def dot(a, b):
    return jnp.dot(a, b, preferred_element_type=F32)


def dot_last(a, b):
    return lax.dot_general(a, b, LAST, preferred_element_type=F32)


def call(body, outs, *args, flops=10**7, moved=10**6, scalars=0):
    vmem = pl.BlockSpec(memory_space=pltpu.VMEM)
    smem = pl.BlockSpec(memory_space=pltpu.SMEM)
    many = isinstance(outs, (tuple, list))
    return pl.pallas_call(
        body,
        out_shape=outs,
        in_specs=[smem] * scalars + [vmem] * (len(args) - scalars),
        out_specs=tuple(vmem for _ in outs) if many else vmem,
        cost_estimate=pl.CostEstimate(flops=flops, bytes_accessed=moved, transcendentals=0),
        compiler_params=pltpu.CompilerParams(vmem_limit_bytes=16 * MIB),
        name=body.__name__,
    )(*args)


def shape(*dims, dtype=BF):
    return jax.ShapeDtypeStruct(dims, dtype)


def lane_order(me):
    i, j = iota((512, 512), 0), iota((512, 512), 1)
    core = jnp.bitwise_xor((i // 64) % 2, me)
    hit = (
        (i // 128 == (j // F) % 4)
        & (core == j // 256)
        & ((i // F) % 2 == (j // 128) % 2)
        & (i % F == j % F)
    )
    return jnp.where(hit, 1.0, 0.0).astype(BF)


def weights_kernel(me_ref, gate_ref, up_ref, down_ref, gu_ref, dn_ref):
    order = lane_order(me_ref[0])
    gu_ref[...] = jnp.zeros_like(gu_ref)
    dn_ref[...] = jnp.zeros_like(dn_ref)
    hidden = gate_ref.shape[0]
    for ref, out, base in ((gate_ref, gu_ref, 0), (up_ref, gu_ref, 128), (down_ref, dn_ref, 0)):
        for xh in range(2):
            for zq in range(4):
                tiles = [
                    ref[:, pl.ds((zq * 4 + zi) * 256 + xh * 128, 128)] for zi in range(4)
                ]
                moved = dot(jnp.concatenate(tiles, axis=1), order).astype(BF)
                for o in range(2):
                    for h in range(2):
                        out[o, xh, pl.ds(base, hidden), pl.ds(h * 512 + zq * 128, 128)] = moved[
                            :, (o * 2 + h) * 128 : (o * 2 + h + 1) * 128
                        ]


def pack_kernel(x_hbm, g_hbm, out_ref, x_ref, g_ref, sems):
    copies = [
        pltpu.make_async_copy(x_hbm, x_ref, sems.at[0]),
        pltpu.make_async_copy(g_hbm, g_ref, sems.at[1]),
    ]
    for copy in copies:
        copy.start()
    for copy in copies:
        copy.wait()
    x = x_ref[...]
    toks, feats = x.shape
    twice = jnp.concatenate([x, x], axis=0)
    keep = iota(twice.shape, 1) // F == iota(twice.shape, 0) // toks
    twice = jnp.where(keep, twice, jnp.zeros_like(twice))
    pick = jnp.where(iota((F, feats), 1) % F == iota((F, feats), 0), 1.0, 0.0).astype(BF)
    x = dot_last(pick, twice).astype(BF)
    blocks = [jnp.concatenate([x, g_ref[F * h : F * (h + 1)]], axis=0) for h in range(2)]
    for z in range(out_ref.shape[0]):
        out_ref[z] = blocks[z % 2]


def placed(routes, rows, capacity, tokens):
    lanes = routes.shape[1]
    expert = iota((rows, lanes), 0) // capacity
    slot = iota((rows, lanes), 0) % capacity
    first, second = routes[0:1, :] == expert, routes[1:2, :] == expert
    named = first | second
    i, j = iota((lanes, lanes), 0), iota((lanes, lanes), 1)
    earlier = jnp.where((i < tokens) & (i < j % tokens), 1.0, 0.0).astype(BF)
    before = dot(jnp.where(named, 1.0, 0.0).astype(BF), earlier)
    return named & (before == slot.astype(F32)), first, second


def named_weights(hit, first, second, gates):
    named = jnp.where(first, gates[0:1, :], 0.0) + jnp.where(second, gates[1:2, :], 0.0)
    return jnp.where(hit, named, 0.0)


def tables_kernel(routes_ref, gates_ref, picks_ref, mix_ref):
    routes, gates = routes_ref[...], gates_ref[...]
    toks = routes.shape[1] // 2
    hit, first, second = placed(routes, picks_ref.shape[1], CAP_B, toks)
    lane = iota(hit.shape, 1) // toks
    for h in range(2):
        picks_ref[h] = jnp.where(hit & (lane == h), 1.0, 0.0).astype(BF)
    weight = named_weights(hit, first, second, gates).T[:toks]
    high = weight.astype(BF)
    rest = weight - high.astype(F32)
    middle = rest.astype(BF)
    mix_ref[0] = high
    mix_ref[1] = middle
    mix_ref[2] = (rest - middle.astype(F32)).astype(BF)


def rows_kernel(picks_ref, routes_ref, gates_ref, got_ref, out_ref):
    experts, _, both, width = out_ref.shape
    slots, half = both // 2, width // 2
    x = got_ref[:, 0:F, :].reshape(-1, picks_ref.shape[2])
    for h in range(2):
        block = dot_last(picks_ref[h], x).astype(BF).reshape(experts, slots, half)
        for xh in range(2):
            out_ref[:, xh, :slots, h * half : (h + 1) * half] = block
    routes, gates = routes_ref[...], gates_ref[...]
    toks = routes.shape[1]
    hit, first, second = placed(routes, experts * 2 * slots, 2 * slots, toks)
    weight = jnp.sum(named_weights(hit, first, second, gates), axis=1, keepdims=True)
    g = got_ref[:, F : 2 * F, :].reshape(-1, toks)
    block = (dot_last(jnp.where(hit, 1.0, 0.0).astype(BF), g) * weight).astype(BF)
    block = block.reshape(experts, 2 * slots, half)
    for xh in range(2):
        out_ref[:, xh, slots:, :half] = block[:, :slots]
        out_ref[:, xh, slots:, half:] = block[:, slots:]


def up_kernel(own_ref, other_ref, gu_ref, dn_ref, hidden_ref, out_ref):
    total = None
    for o, ref in enumerate((own_ref, other_ref)):
        for xh in range(2):
            term = dot_last(rows_of(ref, xh), gu_ref[o, xh])
            total = term if total is None else total + term
    gate, up = total[:, :128], total[:, 128:]
    hidden = (gate / (1.0 + jnp.exp(-gate)) * up).astype(BF)
    hidden_ref[...] = hidden
    groups, _, slots, width = out_ref.shape
    for xh in range(2):
        out_ref[:, xh] = dot(hidden, dn_ref[1, xh]).astype(BF).reshape(groups, slots, width)


def down_kernel(hidden_ref, dn_ref, arrived_ref, out_ref):
    hidden = hidden_ref[...]
    groups, _, slots, width = out_ref.shape
    for xh in range(2):
        total = dot(hidden, dn_ref[0, xh]) + rows_of(arrived_ref, xh).astype(F32)
        out_ref[:, xh] = total.astype(BF).reshape(groups, slots, width)


def mix_kernel(mix_ref, got_ref, out_ref):
    width = got_ref.shape[3] // 2
    parts, toks, rows = mix_ref.shape
    mix = mix_ref[...].reshape(parts * toks, rows)
    halves = []
    for h in range(2):
        total = sum(dot(mix, rows_of(got_ref, xh)[:, h * width : (h + 1) * width]) for xh in range(2))
        halves.append(total[:toks] + total[toks : 2 * toks] + total[2 * toks :])
    mixed = jnp.concatenate(halves, axis=0).T.astype(BF)
    out_ref[...] = mixed.reshape(out_ref.shape)


def total_kernel(got_ref, out_ref):
    total = got_ref[0].astype(F32)
    for z in range(1, got_ref.shape[0]):
        total = total + got_ref[z].astype(F32)
    turned = total.T
    toks = out_ref.shape[0]
    out_ref[...] = jnp.concatenate([turned[:toks], turned[toks:]], axis=1).astype(BF)


def rows_of(ref, xh):
    return ref[:, xh].reshape(-1, ref.shape[3])


def half_rows_of(ref, xh):
    half = ref.shape[3] // 2
    both = jnp.concatenate([ref[:, xh, :, :half], ref[:, xh, :, half:]], axis=1)
    return both.reshape(-1, half)


def back_kernel(
    me_ref, own_ref, near_ref, other_ref, other_near_ref, dn_ref, gate_ref, up_ref,
    down_ref, dg_ref, du_ref, held,
):
    width = own_ref.shape[3] // 2
    mine = pl.ds(pl.multiple_of(me_ref[1] * width, width), width)
    rest = pl.ds(pl.multiple_of((1 - me_ref[1]) * width, width), width)
    parts = ((0, mine, own_ref), (1, mine, other_ref), (0, rest, near_ref), (1, rest, other_near_ref))
    total = None
    for o, lanes, ref in parts:
        for xh in range(2):
            term = dot_last(dn_ref[o, xh, :, lanes], half_rows_of(ref, xh))
            total = term if total is None else total + term
    gate, up = gate_ref[...].astype(F32), up_ref[...].astype(F32)
    grad = total[: gate.shape[0]]
    sigma = 1.0 / (1.0 + jnp.exp(-gate))
    active = gate * sigma
    dg_ref[...] = (grad * up * sigma * (1.0 + gate * (1.0 - sigma))).astype(BF)
    du_ref[...] = (grad * active).astype(BF)
    hidden = (active * up).astype(BF)
    for o, lanes, ref in parts:
        for xh in range(2):
            held[o, xh, :, lanes] = dot(hidden, half_rows_of(ref, xh)).astype(BF)
    order = lane_order(me_ref[0])
    for xh in range(2):
        for zq in range(4):
            tiles = [
                held[o, xh, :, pl.ds(h * 512 + zq * 128, 128)] for o in range(2) for h in range(2)
            ]
            moved = dot_last(jnp.concatenate(tiles, axis=1), order).astype(BF)
            for zi in range(4):
                down_ref[:, pl.ds((zq * 4 + zi) * 256 + xh * 128, 128)] = moved[
                    :, zi * 128 : (zi + 1) * 128
                ]


def other_core(array):
    return lax.ppermute(array, CORE, [(0, 1), (1, 0)])


def exchange(array, axes):
    peers = array.reshape(lax.axis_size(axes), -1, array.shape[-1])
    return lax.all_to_all(peers, axes, 0, 0, tiled=True).reshape(array.shape)


def per_device(
    x_new,
    routes_new,
    gates_new,
    w_gate,
    w_up,
    w_down,
    grad_out,
    routes_old,
    gates_old,
    pre_gate,
    pre_up,
):
    me = jnp.stack([lax.axis_index(CORE), lax.axis_index(Z) % 2]).astype(jnp.int32)
    experts = lax.axis_size(EXPERT)
    rows_new, rows_old = experts * CAP_B, experts * CAP_A
    hidden_units = w_gate.shape[2]
    twice = lambda a: jnp.concatenate([a.T, a.T], axis=1)
    routes_b, gates_b = twice(routes_new), twice(gates_new)
    routes_a, gates_a = routes_old.T, gates_old.T

    packed = pl.pallas_call(
        pack_kernel,
        out_shape=shape(16, 2 * F, 128),
        in_specs=[pl.BlockSpec(memory_space=pltpu.HBM)] * 2,
        out_specs=pl.BlockSpec(memory_space=pltpu.VMEM),
        scratch_shapes=[
            pltpu.VMEM(x_new.shape, BF),
            pltpu.VMEM(grad_out.shape[::-1], BF),
            pltpu.SemaphoreType.DMA((2,)),
        ],
        compiler_params=pltpu.CompilerParams(vmem_limit_bytes=16 * MIB),
        name="pack_kernel",
    )(x_new, grad_out.T)
    got = lax.all_to_all(packed, Z, 0, 0, tiled=True)
    gate_up, down = call(
        weights_kernel,
        (shape(2, 2, 256, 1024), shape(2, 2, 128, 1024)),
        me,
        w_gate[0].T,
        w_up[0].T,
        w_down[0],
        scalars=1,
        flops=14 * 10**8,
        moved=6 * 10**6,
    )

    picks, mix = call(
        tables_kernel,
        (shape(2, rows_new, 128), shape(3, x_new.shape[0], rows_new)),
        routes_b,
        gates_b,
    )
    got, gate_up, down, picks, mix, routes_a, gates_a = lax.optimization_barrier(
        (got, gate_up, down, picks, mix, routes_a, gates_a)
    )

    rows_b = shape(experts, 2, CAP_B, 1024)
    sent = call(
        rows_kernel, shape(experts, 2, 2 * CAP_B, 1024), picks, routes_a, gates_a, got
    )
    arrived = exchange(sent, PLANE)
    own, own_a = arrived[:, :, :CAP_B], arrived[:, :, CAP_B:]

    hidden, partial = call(
        up_kernel,
        (shape(rows_new, 128), rows_b),
        own,
        other_core(own),
        gate_up,
        down,
        flops=8 * 10**8,
        moved=4 * 10**6,
    )
    summed = call(down_kernel, rows_b, hidden, down, other_core(partial), flops=2 * 10**8)
    returned = exchange(summed, PLANE)

    planes, half = lax.axis_size(Z), experts // 2
    near_a = jnp.concatenate(
        [
            lax.ppermute(own_a[:half], Z, [(z, (z + 1) % planes) for z in range(planes)]),
            lax.ppermute(own_a[half:], Z, [(z, (z - 1) % planes) for z in range(planes)]),
        ],
        axis=0,
    )
    other_a, other_near = other_core(own_a), other_core(near_a)
    vmem = pl.BlockSpec(memory_space=pltpu.VMEM)
    weight_grad, gate_grad, up_grad = pl.pallas_call(
        back_kernel,
        out_shape=(
            shape(hidden_units, 4096),
            shape(hidden_units, rows_old),
            shape(hidden_units, rows_old),
        ),
        in_specs=[pl.BlockSpec(memory_space=pltpu.SMEM)] + [vmem] * 7,
        out_specs=(vmem,) * 3,
        scratch_shapes=[pltpu.VMEM((2, 2, hidden_units, 1024), BF)],
        cost_estimate=pl.CostEstimate(
            flops=15 * 10**8, bytes_accessed=8 * 10**6, transcendentals=0
        ),
        compiler_params=pltpu.CompilerParams(vmem_limit_bytes=16 * MIB),
        name="back_kernel",
    )(me, own_a, near_a, other_a, other_near, down, pre_gate[0].T, pre_up[0].T)
    mixed = call(mix_kernel, shape(16, F, 128), mix, returned, flops=4 * 10**8)
    mixed = exchange(mixed, Z)
    mixed, weight_grad, gate_grad, up_grad = lax.optimization_barrier(
        (mixed, weight_grad, gate_grad, up_grad)
    )
    mixed = call(total_kernel, shape(*x_new.shape), mixed)
    return (mixed, weight_grad[None], gate_grad.T[None], up_grad.T[None])


def solution(mesh):
    torus = Mesh(
        mesh.devices.reshape(4, 2, 16, 2, 2), ("expert_0", "expert_1", "dp_0", "dp_1", "dp_2")
    )
    placed_as = (
        P(EXPERT, DP),
        P(EXPERT, None),
        P(EXPERT, None),
        P(EXPERT, None, DP),
        P(EXPERT, None, DP),
        P(EXPERT, DP, None),
        P(EXPERT, DP),
        P(EXPERT, None),
        P(EXPERT, None),
        P(EXPERT, None, DP),
        P(EXPERT, None, DP),
    )
    return jax.shard_map(
        per_device,
        mesh=torus,
        in_specs=placed_as,
        out_specs=(P(EXPERT, DP), P(EXPERT, DP, None), P(EXPERT, None, DP), P(EXPERT, None, DP)),
        check_vma=False,
    )
```

```python
import functools

import jax
import jax.numpy as jnp
from jax import lax
from jax.experimental import pallas as pl
from jax.experimental.pallas import tpu as pltpu
from jax.sharding import Mesh
from jax.sharding import PartitionSpec as P

CAP_B = 32
CAP_A = 64
EXPERT = ("expert_0", "expert_1")
DP = ("dp_0", "dp_1", "dp_2")
Z = "dp_0"
CORE = "dp_2"
PLANE = ("expert_0", "expert_1", "dp_1")
F = 32
BF = jnp.bfloat16
F32 = jnp.float32
LAST = (((1,), (1,)), ((), ()))
MIB = 1 << 20


def iota(shape, dim):
    return lax.broadcasted_iota(jnp.int32, shape, dim)


def dot(a, b):
    return jnp.dot(a, b, preferred_element_type=F32)


def dot_last(a, b):
    return lax.dot_general(a, b, LAST, preferred_element_type=F32)


def call(body, outs, *args, flops=10**7, moved=10**6, scalars=0):
    vmem = pl.BlockSpec(memory_space=pltpu.VMEM)
    smem = pl.BlockSpec(memory_space=pltpu.SMEM)
    many = isinstance(outs, (tuple, list))
    return pl.pallas_call(
        body,
        out_shape=outs,
        in_specs=[smem] * scalars + [vmem] * (len(args) - scalars),
        out_specs=tuple(vmem for _ in outs) if many else vmem,
        cost_estimate=pl.CostEstimate(flops=flops, bytes_accessed=moved, transcendentals=0),
        compiler_params=pltpu.CompilerParams(vmem_limit_bytes=16 * MIB),
        name=body.__name__,
    )(*args)


def shape(*dims, dtype=BF):
    return jax.ShapeDtypeStruct(dims, dtype)


def lane_order(me):
    i, j = iota((512, 512), 0), iota((512, 512), 1)
    core = jnp.bitwise_xor((i // 64) % 2, me)
    hit = (
        (i // 128 == (j // F) % 4)
        & (core == j // 256)
        & ((i // F) % 2 == (j // 128) % 2)
        & (i % F == j % F)
    )
    return jnp.where(hit, 1.0, 0.0).astype(BF)


def weights_kernel(me_ref, gate_ref, up_ref, down_ref, gu_ref, dn_ref):
    order = lane_order(me_ref[0])
    gu_ref[...] = jnp.zeros_like(gu_ref)
    dn_ref[...] = jnp.zeros_like(dn_ref)
    hidden = gate_ref.shape[0]
    for ref, out, base in ((gate_ref, gu_ref, 0), (up_ref, gu_ref, 128), (down_ref, dn_ref, 0)):
        for xh in range(2):
            for zq in range(4):
                tiles = [
                    ref[:, pl.ds((zq * 4 + zi) * 256 + xh * 128, 128)] for zi in range(4)
                ]
                moved = dot(jnp.concatenate(tiles, axis=1), order).astype(BF)
                for o in range(2):
                    for h in range(2):
                        out[o, xh, pl.ds(base, hidden), pl.ds(h * 512 + zq * 128, 128)] = moved[
                            :, (o * 2 + h) * 128 : (o * 2 + h + 1) * 128
                        ]


def pack_kernel(x_ref, g_ref, out_ref):
    x = x_ref[...]
    toks, feats = x.shape
    twice = jnp.concatenate([x, x], axis=0)
    keep = iota(twice.shape, 1) // F == iota(twice.shape, 0) // toks
    twice = jnp.where(keep, twice, jnp.zeros_like(twice))
    pick = jnp.where(iota((F, feats), 1) % F == iota((F, feats), 0), 1.0, 0.0).astype(BF)
    x = dot_last(pick, twice).astype(BF)
    blocks = [jnp.concatenate([x, g_ref[F * h : F * (h + 1)]], axis=0) for h in range(2)]
    for z in range(out_ref.shape[0]):
        out_ref[z] = blocks[z % 2]


def placed(routes, rows, capacity, tokens):
    lanes = routes.shape[1]
    expert = iota((rows, lanes), 0) // capacity
    slot = iota((rows, lanes), 0) % capacity
    first, second = routes[0:1, :] == expert, routes[1:2, :] == expert
    named = first | second
    i, j = iota((lanes, lanes), 0), iota((lanes, lanes), 1)
    earlier = jnp.where((i < tokens) & (i < j % tokens), 1.0, 0.0).astype(BF)
    before = dot(jnp.where(named, 1.0, 0.0).astype(BF), earlier)
    return named & (before == slot.astype(F32)), first, second


def named_weights(hit, first, second, gates):
    named = jnp.where(first, gates[0:1, :], 0.0) + jnp.where(second, gates[1:2, :], 0.0)
    return jnp.where(hit, named, 0.0)


def tables_kernel(routes_ref, gates_ref, picks_ref, mix_ref):
    routes, gates = routes_ref[...], gates_ref[...]
    toks = routes.shape[1] // 2
    hit, first, second = placed(routes, picks_ref.shape[1], CAP_B, toks)
    lane = iota(hit.shape, 1) // toks
    for h in range(2):
        picks_ref[h] = jnp.where(hit & (lane == h), 1.0, 0.0).astype(BF)
    weight = named_weights(hit, first, second, gates).T[:toks]
    high = weight.astype(BF)
    rest = weight - high.astype(F32)
    middle = rest.astype(BF)
    mix_ref[0] = high
    mix_ref[1] = middle
    mix_ref[2] = (rest - middle.astype(F32)).astype(BF)


def rows_kernel(picks_ref, routes_ref, gates_ref, got_ref, out_ref):
    experts, _, both, width = out_ref.shape
    slots, half = both // 2, width // 2
    x = got_ref[:, 0:F, :].reshape(-1, picks_ref.shape[2])
    for h in range(2):
        block = dot_last(picks_ref[h], x).astype(BF).reshape(experts, slots, half)
        for xh in range(2):
            out_ref[:, xh, :slots, h * half : (h + 1) * half] = block
    routes, gates = routes_ref[...], gates_ref[...]
    toks = routes.shape[1]
    hit, first, second = placed(routes, experts * 2 * slots, 2 * slots, toks)
    weight = jnp.sum(named_weights(hit, first, second, gates), axis=1, keepdims=True)
    g = got_ref[:, F : 2 * F, :].reshape(-1, toks)
    block = (dot_last(jnp.where(hit, 1.0, 0.0).astype(BF), g) * weight).astype(BF)
    block = block.reshape(experts, 2 * slots, half)
    for xh in range(2):
        out_ref[:, xh, slots:, :half] = block[:, :slots]
        out_ref[:, xh, slots:, half:] = block[:, slots:]


def up_kernel(own_ref, other_ref, gu_ref, dn_ref, hidden_ref, out_ref):
    total = None
    for o, ref in enumerate((own_ref, other_ref)):
        for xh in range(2):
            term = dot_last(rows_of(ref, xh), gu_ref[o, xh])
            total = term if total is None else total + term
    gate, up = total[:, :128], total[:, 128:]
    hidden = (gate / (1.0 + jnp.exp(-gate)) * up).astype(BF)
    hidden_ref[...] = hidden
    groups, _, slots, width = out_ref.shape
    for xh in range(2):
        out_ref[:, xh] = dot(hidden, dn_ref[1, xh]).astype(BF).reshape(groups, slots, width)


def down_kernel(hidden_ref, dn_ref, arrived_ref, out_ref):
    hidden = hidden_ref[...]
    groups, _, slots, width = out_ref.shape
    for xh in range(2):
        total = dot(hidden, dn_ref[0, xh]) + rows_of(arrived_ref, xh).astype(F32)
        out_ref[:, xh] = total.astype(BF).reshape(groups, slots, width)


def mix_kernel(mix_ref, got_ref, out_ref):
    width = got_ref.shape[3] // 2
    parts, toks, rows = mix_ref.shape
    mix = mix_ref[...].reshape(parts * toks, rows)
    halves = []
    for h in range(2):
        total = sum(dot(mix, rows_of(got_ref, xh)[:, h * width : (h + 1) * width]) for xh in range(2))
        halves.append(total[:toks] + total[toks : 2 * toks] + total[2 * toks :])
    mixed = jnp.concatenate(halves, axis=0).T.astype(BF)
    out_ref[...] = mixed.reshape(out_ref.shape)


def total_kernel(got_ref, out_ref):
    total = got_ref[0].astype(F32)
    for z in range(1, got_ref.shape[0]):
        total = total + got_ref[z].astype(F32)
    turned = total.T
    toks = out_ref.shape[0]
    out_ref[...] = jnp.concatenate([turned[:toks], turned[toks:]], axis=1).astype(BF)


def rows_of(ref, xh):
    return ref[:, xh].reshape(-1, ref.shape[3])


def half_rows_of(ref, xh):
    half = ref.shape[3] // 2
    both = jnp.concatenate([ref[:, xh, :, :half], ref[:, xh, :, half:]], axis=1)
    return both.reshape(-1, half)


def back_kernel(
    me_ref, own_ref, near_ref, other_ref, other_near_ref, dn_ref, gate_ref, up_ref,
    down_ref, dg_ref, du_ref, held,
):
    width = own_ref.shape[3] // 2
    mine = pl.ds(pl.multiple_of(me_ref[1] * width, width), width)
    rest = pl.ds(pl.multiple_of((1 - me_ref[1]) * width, width), width)
    parts = ((0, mine, own_ref), (1, mine, other_ref), (0, rest, near_ref), (1, rest, other_near_ref))
    total = None
    for o, lanes, ref in parts:
        for xh in range(2):
            term = dot_last(dn_ref[o, xh, :, lanes], half_rows_of(ref, xh))
            total = term if total is None else total + term
    gate, up = gate_ref[...].astype(F32), up_ref[...].astype(F32)
    grad = total[: gate.shape[0]]
    sigma = 1.0 / (1.0 + jnp.exp(-gate))
    active = gate * sigma
    dg_ref[...] = (grad * up * sigma * (1.0 + gate * (1.0 - sigma))).astype(BF)
    du_ref[...] = (grad * active).astype(BF)
    hidden = (active * up).astype(BF)
    for o, lanes, ref in parts:
        for xh in range(2):
            held[o, xh, :, lanes] = dot(hidden, half_rows_of(ref, xh)).astype(BF)
    order = lane_order(me_ref[0])
    for xh in range(2):
        for zq in range(4):
            tiles = [
                held[o, xh, :, pl.ds(h * 512 + zq * 128, 128)] for o in range(2) for h in range(2)
            ]
            moved = dot_last(jnp.concatenate(tiles, axis=1), order).astype(BF)
            for zi in range(4):
                down_ref[:, pl.ds((zq * 4 + zi) * 256 + xh * 128, 128)] = moved[
                    :, zi * 128 : (zi + 1) * 128
                ]


def other_core(array):
    return lax.ppermute(array, CORE, [(0, 1), (1, 0)])


def exchange(array, axes):
    peers = array.reshape(lax.axis_size(axes), -1, array.shape[-1])
    return lax.all_to_all(peers, axes, 0, 0, tiled=True).reshape(array.shape)


def per_device(
    x_new,
    routes_new,
    gates_new,
    w_gate,
    w_up,
    w_down,
    grad_out,
    routes_old,
    gates_old,
    pre_gate,
    pre_up,
):
    me = jnp.stack([lax.axis_index(CORE), lax.axis_index(Z) % 2]).astype(jnp.int32)
    experts = lax.axis_size(EXPERT)
    rows_new, rows_old = experts * CAP_B, experts * CAP_A
    hidden_units = w_gate.shape[2]
    twice = lambda a: jnp.concatenate([a.T, a.T], axis=1)
    routes_b, gates_b = twice(routes_new), twice(gates_new)
    routes_a, gates_a = routes_old.T, gates_old.T

    whole = lambda *dims: pl.BlockSpec(dims, lambda i: (0,) * len(dims))
    packed = pl.pallas_call(
        pack_kernel,
        out_shape=shape(16, 2 * F, 128),
        grid=(1,),
        in_specs=[whole(*x_new.shape), whole(*grad_out.shape[::-1])],
        out_specs=whole(16, 2 * F, 128),
        compiler_params=pltpu.CompilerParams(vmem_limit_bytes=16 * MIB),
        name="pack_kernel",
    )(x_new, grad_out.T)
    got = lax.all_to_all(packed, Z, 0, 0, tiled=True)
    gate_up, down = call(
        weights_kernel,
        (shape(2, 2, 256, 1024), shape(2, 2, 128, 1024)),
        me,
        w_gate[0].T,
        w_up[0].T,
        w_down[0],
        scalars=1,
        flops=14 * 10**8,
        moved=6 * 10**6,
    )

    picks, mix = call(
        tables_kernel,
        (shape(2, rows_new, 128), shape(3, x_new.shape[0], rows_new)),
        routes_b,
        gates_b,
    )
    got, gate_up, down, picks, mix, routes_a, gates_a = lax.optimization_barrier(
        (got, gate_up, down, picks, mix, routes_a, gates_a)
    )

    rows_b = shape(experts, 2, CAP_B, 1024)
    sent = call(
        rows_kernel, shape(experts, 2, 2 * CAP_B, 1024), picks, routes_a, gates_a, got
    )
    arrived = exchange(sent, PLANE)
    own = arrived[:, :, :CAP_B]

    hidden, partial = call(
        up_kernel,
        (shape(rows_new, 128), rows_b),
        own,
        other_core(own),
        gate_up,
        down,
        flops=8 * 10**8,
        moved=4 * 10**6,
    )
    arrived, partial = lax.optimization_barrier((arrived, partial))
    own_a = arrived[:, :, CAP_B:]
    summed = call(down_kernel, rows_b, hidden, down, other_core(partial), flops=2 * 10**8)
    returned = exchange(summed, PLANE)

    near_a = lax.ppermute(own_a, Z, [(z, z ^ 1) for z in range(lax.axis_size(Z))])
    other_a, other_near = other_core(own_a), other_core(near_a)
    vmem = pl.BlockSpec(memory_space=pltpu.VMEM)
    weight_grad, gate_grad, up_grad = pl.pallas_call(
        back_kernel,
        out_shape=(
            shape(hidden_units, 4096),
            shape(hidden_units, rows_old),
            shape(hidden_units, rows_old),
        ),
        in_specs=[pl.BlockSpec(memory_space=pltpu.SMEM)] + [vmem] * 7,
        out_specs=(vmem,) * 3,
        scratch_shapes=[pltpu.VMEM((2, 2, hidden_units, 1024), BF)],
        cost_estimate=pl.CostEstimate(
            flops=15 * 10**8, bytes_accessed=8 * 10**6, transcendentals=0
        ),
        compiler_params=pltpu.CompilerParams(vmem_limit_bytes=16 * MIB),
        name="back_kernel",
    )(me, own_a, near_a, other_a, other_near, down, pre_gate[0].T, pre_up[0].T)
    mixed = call(mix_kernel, shape(16, F, 128), mix, returned, flops=4 * 10**8)
    mixed = exchange(mixed, Z)
    mixed, weight_grad, gate_grad, up_grad = lax.optimization_barrier(
        (mixed, weight_grad, gate_grad, up_grad)
    )
    mixed = call(total_kernel, shape(*x_new.shape), mixed)
    return (mixed, weight_grad[None], gate_grad.T[None], up_grad.T[None])


def solution(mesh):
    torus = Mesh(
        mesh.devices.reshape(4, 2, 16, 2, 2), ("expert_0", "expert_1", "dp_0", "dp_1", "dp_2")
    )
    placed_as = (
        P(EXPERT, DP),
        P(EXPERT, None),
        P(EXPERT, None),
        P(EXPERT, None, DP),
        P(EXPERT, None, DP),
        P(EXPERT, DP, None),
        P(EXPERT, DP),
        P(EXPERT, None),
        P(EXPERT, None),
        P(EXPERT, None, DP),
        P(EXPERT, None, DP),
    )
    return jax.shard_map(
        per_device,
        mesh=torus,
        in_specs=placed_as,
        out_specs=(P(EXPERT, DP), P(EXPERT, DP, None), P(EXPERT, None, DP), P(EXPERT, None, DP)),
        check_vma=False,
    )
```
